512 devices in a mesh: dom: 64 (over x, z), sub: 8 (over y, core).
Axes of the slice: x: 4, y: 4, z: 16, core: 2. Of those that a mesh axis runs over, the one named last changes fastest.
Arguments:
- adjoint_in: float32 [4, 27, 262144], P(None, None, ('dom', 'sub')), may hold values from -6 to 6
- viscosity: float32 [27, 262144], P(None, ('dom', 'sub')), may hold values from 0.05 to 1
- velocity: float32 [3, 262144], P(None, ('dom', 'sub')), may hold values from -1 to 1
- inverse_size: float32 [262144], P(('dom', 'sub')), may hold values from 0.5 to 2
- local_partner: int32 [64, 8, 3072], P('dom', 'sub'), may hold values from 0 to 3071, as said below
- face_orient: int32 [64, 8, 3072], P('dom', 'sub'), may hold values from 0 to 7
- dom_counts: int32 [64, 8, 4], P('dom', 'sub'), may hold values from 0 to 256, as said below
- dom_slots: int32 [64, 8, 4, 256], P('dom', 'sub'), may hold values from 0 to 3071, as said below
- sub_slots: int32 [64, 8, 2, 128], P('dom', 'sub'), may hold values from 0 to 3071, as said below
Outputs:
- adjoint_out: float32 [4, 27, 262144], P(None, None, ('dom', 'sub'))
The draws below stay inside these ranges and needn't reach their ends.
Inputs may be any that keep to these rules, and one draw needn't show every extreme that they name: For each device and offset index l: dom_counts[l] equals dom_counts[3 - l] of the device at that offset along dom, and is 0 where that device does not exist. Between partitions next to each other the count is at least 128 and 256 is reached in every draw; at offsets -2 and +2 it is at most 64, which is reached in every draw. Face slots of the device; the entries of dom_slots and sub_slots of one device are all distinct; entries at positions of the count or beyond name slots whose local_partner is the slot itself. `sub_slots`: face slots of the device, distinct from each other and from those in dom_slots. `local_partner`: on each device a pairing of face slots (partner of partner is the slot), equal to the slot itself on every slot named in dom_slots or sub_slots.
All inputs are finite; a program needn't handle non-finite values.
Results may differ from the reference program's by a relative error of at most 0.0003.
Values sent between devices are 32-bit elements; how exact they have to be, the bound alone decides.
A program may use at most 64 MiB of HBM per device.

```python
import math
import jax
import jax.numpy as jnp
import numpy as np
from jax import lax

VARIABLES = 4
NODES = 27
ELEM_DEV = 512
NEAR_CAP = 256
FAR_CAP = 64
SECTOR_CAP = 128
ELEMENTS = 262144
N_DOM = 64
N_SUB = 8


def slot_orders(key):
    device_count = N_DOM * N_SUB
    slot_count = 6 * ELEM_DEV
    keys = jax.random.split(jax.random.fold_in(key, 11), device_count)

    def permute_one(single_key):
        return jax.random.permutation(single_key, slot_count)
    return jax.vmap(permute_one)(keys).astype(jnp.int32)


def draw_dom_counts(key, part):
    near_key = jax.random.fold_in(key, 21)
    far_key = jax.random.fold_in(key, 22)
    closest_upper_key = jax.random.fold_in(key, 23)
    far_top_key = jax.random.fold_in(key, 24)
    near = jax.random.randint(near_key, (N_DOM, N_SUB), NEAR_CAP // 2, NEAR_CAP + 1)
    far = jax.random.randint(far_key, (N_DOM, N_SUB), 0, FAR_CAP + 1)
    near_top = jax.random.randint(closest_upper_key, (N_SUB,), 0, N_DOM - 1)
    far_top = jax.random.randint(far_top_key, (N_SUB,), 0, N_DOM - 2)
    rows = jnp.arange(N_DOM)[:, None]
    near = jnp.where(rows == near_top[None, :], NEAR_CAP, near)
    far = jnp.where(rows == far_top[None, :], FAR_CAP, far)
    near = jnp.where(rows <= N_DOM - 2, near, 0)
    far = jnp.where(rows <= N_DOM - 3, far, 0)
    minus_two = jnp.roll(far, 2, axis=0)
    minus_one = jnp.roll(near, 1, axis=0)
    return jnp.stack([minus_two, minus_one, near, far], axis=2).astype(jnp.int32)


def draw_dom_slots(key, part):
    orders = slot_orders(key)
    return orders[:, :4 * NEAR_CAP].reshape(N_DOM, N_SUB, 4, NEAR_CAP)


def draw_sub_slots(key, part):
    orders = slot_orders(key)
    return orders[:, 4 * NEAR_CAP:4 * NEAR_CAP + 2 * SECTOR_CAP].reshape(N_DOM, N_SUB, 2, SECTOR_CAP)


def draw_local_partner(key, part):
    orders = slot_orders(key)
    slot_count = 6 * ELEM_DEV
    reserved = 4 * NEAR_CAP + 2 * SECTOR_CAP

    def pair_one(order_row):
        leftover = order_row[reserved:]
        start = jnp.arange(slot_count, dtype=jnp.int32)
        return start.at[leftover[0::2]].set(leftover[1::2]).at[leftover[1::2]].set(leftover[0::2])
    return jax.vmap(pair_one)(orders).reshape(N_DOM, N_SUB, slot_count).astype(jnp.int32)


def with_ends(values, stream_key, low, high):
    dims = values.shape
    spot = [jax.random.randint(jax.random.fold_in(stream_key, axis), (), 0, dims[axis]) for axis in range(len(dims))]
    values = values.at[tuple(spot)].set(low)
    longest = dims.index(max(dims))
    spot[longest] = (spot[longest] + 1) % dims[longest]
    return values.at[tuple(spot)].set(high)


def block_levels(key, dims, pieces, smallest, top_value):
    loudness, own = 1.0, jax.random.fold_in(key, 6)
    for axis_at, blocks in pieces:
        steps = jnp.exp(jax.random.uniform(jax.random.fold_in(own, axis_at), (blocks,), jnp.float32, smallest / len(pieces), top_value / len(pieces)))
        loudness = loudness * jnp.repeat(steps, dims[axis_at] // blocks).reshape([-1 if axis == axis_at else 1 for axis in range(len(dims))])
    return loudness


def centred(rng, shape, spread, reach, cuts=(), kind=jnp.bfloat16):
    values = jax.random.normal(rng, shape, jnp.float32) * spread
    if len(cuts) > 0:
        values = block_levels(rng, shape, cuts, -0.22, 0.18) * values
    return jnp.clip(values, min=-reach, max=reach).astype(kind)


def setup_inputs(seed: int = 0) -> dict:
    key_of = jax.random.split(jax.random.key(seed), 10)
    return {
        "adjoint_in": centred(key_of[0], (VARIABLES, NODES, ELEMENTS), 1.0, 6.0, ((2, 512),), jnp.float32),
        "viscosity": jnp.clip(jnp.exp(math.log(1.0) - 2.9957323 * jax.random.uniform(key_of[1], (NODES, ELEMENTS), jnp.float32) ** block_levels(key_of[1], (NODES, ELEMENTS), ((1, 512),), -0.2, 0.2)), 0.05, 1.0),
        "velocity": jnp.clip(jax.random.uniform(key_of[2], (3, ELEMENTS), jnp.float32, -1.0, 1.0) * block_levels(key_of[2], (3, ELEMENTS), ((1, 512),), -0.4, 0.0), -1.0, 1.0),
        "inverse_size": jnp.clip(jnp.exp(math.log(2.0) - 1.3862944 * jax.random.uniform(key_of[3], (ELEMENTS,), jnp.float32) ** block_levels(key_of[3], (ELEMENTS,), ((0, 512),), -0.2, 0.2)), 0.5, 2.0),
        "local_partner": draw_local_partner(jax.random.fold_in(key_of[9], 71), 0),
        "face_orient": with_ends(jax.random.randint(key_of[5], (N_DOM, N_SUB, 6 * ELEM_DEV), 0, 8), jax.random.fold_in(key_of[5], 1), 0, 7).astype(jnp.int32),
        "dom_counts": draw_dom_counts(jax.random.fold_in(key_of[9], 71), 0),
        "dom_slots": draw_dom_slots(jax.random.fold_in(key_of[9], 71), 0),
        "sub_slots": draw_sub_slots(jax.random.fold_in(key_of[9], 71), 0),
    }


time_step = 0.02
penalty = 2.0
offsets = (-2, -1, 1, 2)

def element_tables():
    points = np.array([-np.sqrt(0.6), 0.0, np.sqrt(0.6)])
    weights = np.array([5.0, 8.0, 5.0]) / 9.0

    def lagrange(node_position):
        field_values = np.ones(3)
        for j in range(3):
            for m in range(3):
                if m != j:
                    field_values[j] *= (node_position - points[m]) / (points[j] - points[m])
        return field_values
    derivative = np.zeros((3, 3))
    for i in range(3):
        for j in range(3):
            summed = 0.0
            for k in range(3):
                if k != j:
                    scale_factor = 1.0 / (points[j] - points[k])
                    for m in range(3):
                        if m != j and m != k:
                            scale_factor *= (points[i] - points[m]) / (points[j] - points[m])
                    summed += scale_factor
            derivative[i, j] = summed
    end_values = (lagrange(-1.0), lagrange(1.0))
    identity = np.eye(3)
    per_axis = [np.kron(np.kron(derivative, identity), identity), np.kron(np.kron(identity, derivative), identity), np.kron(np.kron(identity, identity), derivative)]
    to_faces = np.zeros((54, 27))
    normals = np.zeros(54)
    face_axis = np.zeros(54, dtype=np.int64)
    face_weight = np.zeros(54)
    for d in range(3):
        others = [a for a in range(3) if a != d]
        for s in range(2):
            for i in range(3):
                for j in range(3):
                    row_id = (i * 3 + j) * 6 + 2 * d + s
                    normals[row_id] = 2.0 * s - 1.0
                    face_axis[row_id] = d
                    face_weight[row_id] = weights[i] * weights[j]
                    for k in range(3):
                        corner = [0, 0, 0]
                        corner[d] = k
                        corner[others[0]] = i
                        corner[others[1]] = j
                        to_faces[row_id, corner[0] * 9 + corner[1] * 3 + corner[2]] = end_values[s][k]
    volume_weight = np.kron(np.kron(weights, weights), weights)
    lifting = (to_faces * face_weight[:, None]).T / volume_weight[:, None]
    lift_grad = np.zeros((81, 54))
    normal_map = np.zeros((54, 81))
    for d in range(3):
        signed = normals * (face_axis == d)
        lift_grad[d * 27:(d + 1) * 27] = lifting * signed[None, :] * 0.5
        normal_map[:, d * 27:(d + 1) * 27] = to_faces * signed[:, None]
    first_map = np.concatenate(per_axis + [to_faces], 0)
    final_map = np.concatenate(per_axis + [lifting], 1)
    turn_table = np.zeros((8, 9), dtype=np.int32)
    for c in range(8):
        for i in range(3):
            for j in range(3):
                row_pos, col_pos = (j, i) if c & 4 else (i, j)
                if c & 1:
                    row_pos = 2 - row_pos
                if c & 2:
                    col_pos = 2 - col_pos
                turn_table[c, i * 3 + j] = row_pos * 3 + col_pos
    return (first_map, lift_grad, normal_map, final_map, turn_table, volume_weight)

def highest(operator_matrix, field_values):
    return jnp.einsum('ba,hat->hbt', operator_matrix, field_values, precision=lax.Precision.HIGHEST)

def finish(lam, grads, jump, own_normal, other_normal, inverse, viscosity, velocity, final_map, volume_weight):
    axis_speed = jnp.repeat(velocity, 27, axis=0)
    fluxes = jnp.tile(viscosity, (3, 1))[None] * grads - axis_speed[None] * jnp.tile(lam, (1, 3, 1))
    mean_visc = jnp.einsum('n,ne->e', volume_weight, viscosity, precision=lax.Precision.HIGHEST) / 8.0
    outward = jnp.asarray(np.tile(np.array([-1.0, 1.0, -1.0, 1.0, -1.0, 1.0]), 9), jnp.float32)
    normal_speed = -jnp.tile(jnp.repeat(velocity, 2, axis=0), (9, 1)) * outward[:, None]
    face_rate = jnp.minimum(normal_speed, 0.0) + penalty * (mean_visc * inverse)[None, :]
    surface = face_rate[None] * jump - 0.5 * mean_visc[None, None, :] * (own_normal + other_normal)
    return inverse[None, None, :] * highest(final_map, jnp.concatenate([fluxes, surface], 1))

def reference(adjoint_in, viscosity, velocity, inverse_size, local_partner, face_orient, dom_counts, dom_slots, sub_slots):
    tables = element_tables()
    first_map, lift_grad, normal_map, final_map = [jnp.asarray(t, jnp.float32) for t in tables[:4]]
    turn_table = jnp.asarray(tables[4], jnp.int32)
    volume_weight = jnp.asarray(tables[5], jnp.float32)
    device_count = N_DOM * N_SUB
    slot_count = 6 * ELEM_DEV
    block_size = 4 * 9 * slot_count

    def blocks(field_values):
        return jnp.moveaxis(field_values.reshape(field_values.shape[:-1] + (device_count, ELEM_DEV)), -2, 0)
    lam_start = blocks(adjoint_in)
    visc_blocks = blocks(viscosity)
    speed_blocks = blocks(velocity)
    inverse_blocks = inverse_size.reshape(device_count, ELEM_DEV)
    device = jnp.arange(device_count, dtype=jnp.int32).reshape(N_DOM, N_SUB)
    source = device[:, :, None] * slot_count + local_partner
    dom_rows = jnp.arange(N_DOM, dtype=jnp.int32)[:, None, None]
    sub_rows = jnp.arange(N_SUB, dtype=jnp.int32)[None, :, None]
    places = jnp.arange(NEAR_CAP, dtype=jnp.int32)[None, None, :]
    for i in range(4):
        shifted = -offsets[i]
        theirs = jnp.roll(device, shifted, axis=0)[:, :, None] * slot_count + jnp.roll(dom_slots[:, :, 3 - i, :], shifted, axis=0)
        target = jnp.where(places < dom_counts[:, :, i:i + 1], dom_slots[:, :, i, :], slot_count)
        source = source.at[dom_rows, sub_rows, target].set(theirs, mode='drop')
    for j, shifted in ((0, 1), (1, -1)):
        theirs = jnp.roll(device, shifted, axis=1)[:, :, None] * slot_count + jnp.roll(sub_slots[:, :, 1 - j, :], shifted, axis=1)
        source = source.at[dom_rows, sub_rows, sub_slots[:, :, j, :]].set(theirs)
    source_dev = source // slot_count
    source_slot = source % slot_count
    rotated_values = jnp.moveaxis(turn_table[face_orient], -1, 2)
    collect_index = (source_dev[:, :, None, :] * block_size + rotated_values * slot_count + source_slot[:, :, None, :]).reshape(device_count, 9, slot_count)
    component_start = (jnp.arange(4, dtype=jnp.int32) * (9 * slot_count))[:, None]

    def fetch(flat_all, index):
        return jnp.take(flat_all, index.reshape(1, -1) + component_start).reshape(4, 54, ELEM_DEV)

    def residual(lam):

        def trace_one(single):
            return highest(first_map[81:], single)
        own = lax.map(trace_one, lam)
        own_flat = own.reshape(-1)

        def grads_of(single, inverse, jump):
            return inverse[None, None, :] * (highest(first_map[:81], single) + highest(lift_grad, jump))

        def normal_one(packed):
            single, inverse, index, mine = packed
            jump = fetch(own_flat, index) - mine
            return highest(normal_map, grads_of(single, inverse, jump))
        normal_all = lax.map(normal_one, (lam, inverse_blocks, collect_index, own))
        normal_flat = normal_all.reshape(-1)

        def final_one(packed):
            single, inverse, index, mine, own_normal, visc, speed = packed
            jump = fetch(own_flat, index) - mine
            grads = grads_of(single, inverse, jump)
            return finish(single, grads, jump, own_normal, fetch(normal_flat, index), inverse, visc, speed, final_map, volume_weight)
        return lax.map(final_one, (lam, inverse_blocks, collect_index, own, normal_all, visc_blocks, speed_blocks))
    first_segment = lam_start + time_step * residual(lam_start)
    result = 0.5 * (lam_start + first_segment + time_step * residual(first_segment))
    return jnp.moveaxis(result, 0, -2).reshape(4, 27, device_count * ELEM_DEV)
```

```python
import functools

import jax
import jax.numpy as jnp
import numpy as np
from jax import lax
from jax.experimental import pallas as pl
from jax.experimental.pallas import tpu as pltpu
from jax.sharding import PartitionSpec as P

MESH = pl.DeviceIdType.MESH
STEP = 0.02
F32 = jnp.float32
I32 = jnp.int32


def line_tables():
    points = np.array([-np.sqrt(0.6), 0.0, np.sqrt(0.6)])
    weights = np.array([5.0, 8.0, 5.0]) / 9.0

    def lagrange(at):
        values = np.ones(3)
        for j in range(3):
            for m in range(3):
                if m != j:
                    values[j] *= (at - points[m]) / (points[j] - points[m])
        return values

    derivative = np.zeros((3, 3))
    for i in range(3):
        for j in range(3):
            for k in range(3):
                if k != j:
                    term = 1.0 / (points[j] - points[k])
                    for m in range(3):
                        if m != j and m != k:
                            term *= (points[i] - points[m]) / (points[j] - points[m])
                    derivative[i, j] += term
    derivative[1, 1] = 0.0
    return derivative, (lagrange(-1.0), lagrange(1.0)), weights


DERIV, ENDS, WEIGHTS = line_tables()
SIGNS = (-1.0, 1.0)


def node(d, k, q):
    i, j = divmod(q, 3)
    at = [i, j]
    at.insert(d, k)
    return 9 * at[0] + 3 * at[1] + at[2]


def combine(coefficients, values):
    total = None
    for a, x in zip(coefficients, values):
        a = float(a)
        if a == 0.0:
            continue
        term = x if a == 1.0 else x * a
        total = term if total is None else total + term
    return total


def lanes(x, index):
    return jnp.take_along_axis(x, index, axis=1)


def kernel(
    n_dom,
    n_sub,
    lam_ref,
    visc_ref,
    vel_ref,
    inv_ref,
    part_ref,
    orient_ref,
    cnt_ref,
    dom_ref,
    sub_ref,
    out_ref,
    xs,
    vb,
    velb,
    invb,
    hmv,
    rate,
    tab,
    tp,
    jmp,
    nsum,
    grd,
    ehi,
    elo,
    ihi,
    ilo,
    rhi,
    rlo,
    ori,
    nat,
    dup,
    snear,
    ssub,
    sfar,
    rnear,
    rsub,
    rfar,
    send_sem,
    recv_sem,
):
    dom = lax.axis_index("dom")
    sub = lax.axis_index("sub")

    def at_dom(by):
        return (lax.rem(dom + by + n_dom, n_dom), sub)

    def at_sub(by):
        return (dom, lax.rem(sub + by + n_sub, n_sub))

    barrier = pltpu.get_barrier_semaphore()
    for who in (at_dom(-2), at_dom(2), at_dom(-1), at_dom(1), at_sub(-1), at_sub(1)):
        pl.semaphore_signal(barrier, inc=1, device_id=who, device_id_type=MESH)

    row = lax.broadcasted_iota(I32, (8, 128), 0)
    lane = lax.broadcasted_iota(I32, (8, 128), 1)
    low = row < 4
    half = jnp.where(low, 0, 1)
    left = lane < 64

    def spread(ref, r):
        return jnp.broadcast_to(ref[pl.ds(r, 1), :], (8, 128))

    def halves(ref, r, c):
        a = ref[pl.ds(r, 1), pl.ds(128 * c, 128)]
        b = ref[pl.ds(r, 1), pl.ds(256 + 128 * c, 128)]
        return jnp.where(low, jnp.broadcast_to(a, (8, 128)), jnp.broadcast_to(b, (8, 128)))

    for c in range(2):
        for n in range(27):
            xs[0, c, n] = lam_ref[c, n]
        mean = None
        for n in range(27):
            v = halves(visc_ref, n, c)
            vb[c, n] = v
            w = float(WEIGHTS[n // 9] * WEIGHTS[n // 3 % 3] * WEIGHTS[n % 3])
            mean = v * w if mean is None else mean + v * w
        mean = mean * 0.125
        inv = halves(inv_ref, 0, c)
        invb[c] = inv
        hmv[c] = 0.5 * mean
        for d in range(3):
            speed = halves(vel_ref, d, c)
            velb[c, d] = speed
            for s in range(2):
                outward = speed if s == 0 else -speed
                rate[2 * (2 * d + s) + c] = jnp.minimum(outward, 0.0) + 2.0 * (mean * inv)

    def entries(k):
        if k < 4:
            a = dom_ref[pl.ds(1 + k // 2, 1), pl.ds(128 * (k % 2), 128)]
            return jnp.broadcast_to(a, (8, 128))
        if k < 6:
            return jnp.broadcast_to(sub_ref[pl.ds(k - 4, 1), :], (8, 128))
        a = jnp.broadcast_to(dom_ref[pl.ds(0, 1), pl.ds(0, 128)], (8, 128))
        b = jnp.broadcast_to(dom_ref[pl.ds(3, 1), pl.ds(0, 128)], (8, 128))
        return jnp.where(left, a, pltpu.roll(b, 64, 1))

    def valid(k):
        if k < 4:
            return lane + 128 * (k % 2) < cnt_ref[1 + k // 2]
        if k < 6:
            return lane >= 0
        return jnp.where(left, lane, lane - 64) < jnp.where(left, cnt_ref[0], cnt_ref[3])

    wide = lax.broadcasted_iota(I32, (128, 128), 0)
    found = jnp.zeros((48, 128), F32)
    for k in range(7):
        e = entries(k)
        hi = lax.shift_right_logical(e, 7)
        lo = lax.bitwise_and(e, 127)
        ehi[k] = hi
        elo[k] = lo
        ok = valid(k)
        where_row = [jnp.where((hi == row + 8 * b) & ok, 1.0, 0.0) for b in range(3)]
        lane_f = lane.astype(F32)
        left_rows = [x * float(k + 1) for x in where_row] + [x * lane_f for x in where_row]
        a = jnp.concatenate(left_rows, axis=0).astype(jnp.bfloat16)
        b = jnp.where(jnp.concatenate([lo] * 16, axis=0) == wide, 1.0, 0.0).astype(jnp.bfloat16)
        found = found + lax.dot_general(
            a, b, (((1,), (1,)), ((), ())), preferred_element_type=F32
        )
    nat[...] = found.astype(I32)

    for f in range(6):
        for c in range(2):
            g = 2 * f + c
            ra, rb = 4 * f + c, 4 * f + 2 + c
            p = jnp.where(low, spread(part_ref, ra), spread(part_ref, rb))
            r = lax.shift_right_logical(p, 7)
            other = lax.bitwise_and(lax.shift_right_logical(r, 1), 1)
            swap = lax.bitwise_xor(other, half)
            ihi[g] = swap * 12 + lax.shift_right_logical(r, 2) * 2 + lax.bitwise_and(r, 1)
            ilo[g] = lax.bitwise_and(p, 127)
            rhi[g] = jnp.where(low, spread(nat, ra), spread(nat, rb))
            rlo[g] = jnp.where(low, spread(nat, 24 + ra), spread(nat, 24 + rb))
            ori[g] = jnp.where(low, spread(orient_ref, ra), spread(orient_ref, rb))

    pl.semaphore_wait(barrier, 6)

    def put_table(f, c, values):
        g = 2 * f + c
        swapped = [pltpu.roll(x, 4, 0) for x in values]
        for q in range(9):
            tab[g, q] = values[q]
            tab[12 + g, q] = swapped[q]
        for k in range(5):
            if k < 4:
                tp[4 * f + c, k] = jnp.where(low, values[2 * k], swapped[2 * k + 1])
                tp[4 * f + 2 + c, k] = jnp.where(low, swapped[2 * k], values[2 * k + 1])
            else:
                tp[4 * f + c, k] = values[8]
                tp[4 * f + 2 + c, k] = swapped[8]

    def copies(rnd):
        plan = (
            (sfar.at[rnd, 0], rfar.at[rnd, 1], at_dom(-2)),
            (sfar.at[rnd, 1], rfar.at[rnd, 0], at_dom(2)),
            (snear.at[rnd, 0], rnear.at[rnd, 1], at_dom(-1)),
            (snear.at[rnd, 1], rnear.at[rnd, 0], at_dom(1)),
            (ssub.at[rnd, 0], rsub.at[rnd, 1], at_sub(-1)),
            (ssub.at[rnd, 1], rsub.at[rnd, 0], at_sub(1)),
        )
        return [
            pltpu.make_async_remote_copy(
                src_ref=src,
                dst_ref=dst,
                send_sem=send_sem.at[rnd, i],
                recv_sem=recv_sem.at[rnd, i],
                device_id=who,
                device_id_type=MESH,
            )
            for i, (src, dst, who) in enumerate(plan)
        ]

    def collect(k):
        hi, lo = ehi[k], elo[k]
        total = [None] * 5
        for s in range(24):
            here = hi == s
            for m in range(5):
                x = lanes(tp[s, m], lo)
                total[m] = x if s == 0 else jnp.where(here, x, total[m])
        return total

    def send(rnd):
        out = copies(rnd)
        x = collect(6)
        for m in range(3):
            a = x[2 * m]
            if m < 2:
                b = x[2 * m + 1]
                sfar[rnd, 0, m] = jnp.where(left, a, pltpu.roll(b, 64, 1))
                sfar[rnd, 1, m] = jnp.where(left, pltpu.roll(a, 64, 1), b)
            else:
                sfar[rnd, 0, m] = a
                sfar[rnd, 1, m] = pltpu.roll(a, 64, 1)
        out[0].start()
        out[1].start()
        for side in range(2):
            for part in range(2):
                x = collect(2 * side + part)
                for m in range(5):
                    snear[rnd, side, 5 * part + m] = x[m]
            out[2 + side].start()
        for side in range(2):
            x = collect(4 + side)
            for m in range(5):
                ssub[rnd, side, m] = x[m]
            out[4 + side].start()

    def local(into):
        def groups(b, carry):
            for u in range(4):
                g = 4 * b + u
                hi, lo = ihi[g], ilo[g]
                total = [None] * 9
                for s in range(24):
                    here = hi == s
                    for q in range(9):
                        x = lanes(tab[s, q], lo)
                        total[q] = x if s == 0 else jnp.where(here, x, total[q])
                for q in range(9):
                    into[g, q] = total[q]
            return carry

        lax.fori_loop(0, 3, groups, 0)

    def arrive(rnd, into, difference):
        for copy in copies(rnd):
            copy.wait()
        lists = [[rnear[rnd, k // 2, 5 * (k % 2) + m] for m in range(5)] for k in range(4)]
        lists += [[rsub[rnd, k, m] for m in range(5)] for k in range(2)]
        far = []
        for m in range(3):
            a, b = rfar[rnd, 0, m], rfar[rnd, 1, m]
            far.append(jnp.where(left, a, pltpu.roll(b, 64, 1)))
            if m < 2:
                far.append(jnp.where(left, pltpu.roll(a, 64, 1), b))
        lists.append(far)
        for k in range(7):
            for m in range(5):
                x = lists[k][m]
                y = pltpu.roll(x, 4, 0)
                dup[k, 2 * m] = jnp.where(low, x, y)
                if m < 4:
                    dup[k, 2 * m + 1] = jnp.where(low, y, x)

        def groups(b, carry):
            for u in range(4):
                g = 4 * b + u
                hi, lo, code = rhi[g], rlo[g], ori[g]
                total = [into[g, q] for q in range(9)]
                for k in range(7):
                    here = hi == k + 1
                    for q in range(9):
                        total[q] = jnp.where(here, lanes(dup[k, q], lo), total[q])
                flip_i = lax.bitwise_and(code, 1) == 1
                flip_j = lax.bitwise_and(code, 2) == 2
                swap = lax.bitwise_and(code, 4) == 4
                for j in range(3):
                    a, b2 = total[j], total[6 + j]
                    total[j] = jnp.where(flip_i, b2, a)
                    total[6 + j] = jnp.where(flip_i, a, b2)
                for i in range(3):
                    a, b2 = total[3 * i], total[3 * i + 2]
                    total[3 * i] = jnp.where(flip_j, b2, a)
                    total[3 * i + 2] = jnp.where(flip_j, a, b2)
                for i in range(3):
                    for j in range(i):
                        a, b2 = total[3 * i + j], total[3 * j + i]
                        total[3 * i + j] = jnp.where(swap, b2, a)
                        total[3 * j + i] = jnp.where(swap, a, b2)
                for q in range(9):
                    own = tab[g, q]
                    into[g, q] = total[q] - own if difference else total[q] + own
            return carry

        lax.fori_loop(0, 3, groups, 0)

    def segment(seg, carry):
        def traces(c, carry):
            for d in range(3):
                face = ([], [])
                for q in range(9):
                    x = [xs[seg, c, node(d, k, q)] for k in range(3)]
                    for s in range(2):
                        face[s].append(combine(ENDS[s], x))
                for s in range(2):
                    put_table(2 * d + s, c, face[s])
            return carry

        lax.fori_loop(0, 2, traces, 0)
        send(2 * seg)
        local(jmp)
        arrive(2 * seg, jmp, True)

        def gradients(c, carry):
            inv = invb[c]
            for d in range(3):
                face = ([], [])
                for q in range(9):
                    x = [xs[seg, c, node(d, k, q)] for k in range(3)]
                    jumps = [jmp[2 * (2 * d + s) + c, q] for s in range(2)]
                    g = []
                    for k in range(3):
                        lift = [0.5 * SIGNS[s] * ENDS[s][k] / WEIGHTS[k] for s in range(2)]
                        g.append(inv * combine(list(DERIV[k]) + lift, x + jumps))
                        grd[c, d, 3 * q + k] = g[k]
                    for s in range(2):
                        face[s].append(combine(SIGNS[s] * ENDS[s], g))
                for s in range(2):
                    put_table(2 * d + s, c, face[s])
            return carry

        lax.fori_loop(0, 2, gradients, 0)
        send(2 * seg + 1)
        local(nsum)
        arrive(2 * seg + 1, nsum, False)

        def advance(c, carry):
            inv, drag = invb[c], hmv[c]
            total = [None] * 27
            for d in range(3):
                speed = velb[c, d]
                rates = [rate[2 * (2 * d + s) + c] for s in range(2)]
                for q in range(9):
                    flux = []
                    for k in range(3):
                        n = node(d, k, q)
                        flux.append(vb[c, n] * grd[c, d, 3 * q + k] - speed * xs[seg, c, n])
                    surface = []
                    for s in range(2):
                        g = 2 * (2 * d + s) + c
                        surface.append(rates[s] * jmp[g, q] - drag * nsum[g, q])
                    for k in range(3):
                        n = node(d, k, q)
                        lift = [ENDS[s][k] / WEIGHTS[k] for s in range(2)]
                        term = combine(list(DERIV[k]) + lift, flux + surface)
                        total[n] = term if total[n] is None else total[n] + term
            scale = STEP * inv
            for n in range(27):
                new = xs[seg, c, n] + scale * total[n]
                xs[seg + 1, c, n] = new
                out_ref[c, n] = 0.5 * (xs[0, c, n] + new)
            return carry

        lax.fori_loop(0, 2, advance, 0)
        return carry

    lax.fori_loop(0, 2, segment, 0)


def on_device(
    n_dom,
    n_sub,
    adjoint_in,
    viscosity,
    velocity,
    inverse_size,
    local_partner,
    face_orient,
    dom_counts,
    dom_slots,
    sub_slots,
):
    lam = adjoint_in.reshape(4, 27, 2, 2, 128).transpose(3, 1, 2, 0, 4).reshape(2, 27, 8, 128)
    vmem = pl.BlockSpec(memory_space=pltpu.VMEM)
    smem = pl.BlockSpec(memory_space=pltpu.SMEM)
    tile = (8, 128)
    out = pl.pallas_call(
        functools.partial(kernel, n_dom, n_sub),
        out_shape=jax.ShapeDtypeStruct((2, 27, 8, 128), F32),
        in_specs=[vmem] * 6 + [smem] + [vmem] * 2,
        out_specs=vmem,
        scratch_shapes=[
            pltpu.VMEM((3, 2, 27) + tile, F32),
            pltpu.VMEM((2, 27) + tile, F32),
            pltpu.VMEM((2, 3) + tile, F32),
            pltpu.VMEM((2,) + tile, F32),
            pltpu.VMEM((2,) + tile, F32),
            pltpu.VMEM((12,) + tile, F32),
            pltpu.VMEM((24, 9) + tile, F32),
            pltpu.VMEM((24, 5) + tile, F32),
            pltpu.VMEM((12, 9) + tile, F32),
            pltpu.VMEM((12, 9) + tile, F32),
            pltpu.VMEM((2, 3, 27) + tile, F32),
            pltpu.VMEM((7,) + tile, I32),
            pltpu.VMEM((7,) + tile, I32),
            pltpu.VMEM((12,) + tile, I32),
            pltpu.VMEM((12,) + tile, I32),
            pltpu.VMEM((12,) + tile, I32),
            pltpu.VMEM((12,) + tile, I32),
            pltpu.VMEM((12,) + tile, I32),
            pltpu.VMEM((48, 128), I32),
            pltpu.VMEM((7, 9) + tile, F32),
            pltpu.VMEM((4, 2, 10) + tile, F32),
            pltpu.VMEM((4, 2, 5) + tile, F32),
            pltpu.VMEM((4, 2, 3) + tile, F32),
            pltpu.VMEM((4, 2, 10) + tile, F32),
            pltpu.VMEM((4, 2, 5) + tile, F32),
            pltpu.VMEM((4, 2, 3) + tile, F32),
            pltpu.SemaphoreType.DMA((4, 6)),
            pltpu.SemaphoreType.DMA((4, 6)),
        ],
        compiler_params=pltpu.CompilerParams(collective_id=0, has_side_effects=True),
        name="segments",
    )(
        lam,
        viscosity,
        velocity,
        inverse_size.reshape(1, 512),
        local_partner.reshape(24, 128),
        face_orient.reshape(24, 128),
        dom_counts.reshape(4),
        dom_slots.reshape(4, 256),
        sub_slots.reshape(2, 128),
    )
    return out.reshape(2, 27, 2, 4, 128).transpose(3, 1, 2, 0, 4).reshape(4, 27, 512)


def solution(mesh):
    in_specs = (
        P(None, None, ("dom", "sub")),
        P(None, ("dom", "sub")),
        P(None, ("dom", "sub")),
        P(("dom", "sub")),
        P("dom", "sub", None),
        P("dom", "sub", None),
        P("dom", "sub", None),
        P("dom", "sub", None, None),
        P("dom", "sub", None, None),
    )
    return jax.shard_map(
        functools.partial(on_device, mesh.shape["dom"], mesh.shape["sub"]),
        mesh=mesh,
        in_specs=in_specs,
        out_specs=P(None, None, ("dom", "sub")),
        check_vma=False,
    )
```

```python
import functools

import jax
import jax.numpy as jnp
import numpy as np
from jax import lax
from jax.experimental import pallas as pl
from jax.experimental.pallas import tpu as pltpu
from jax.sharding import PartitionSpec as P

MESH = pl.DeviceIdType.MESH
STEP = 0.02
F32 = jnp.float32
I32 = jnp.int32


def line_tables():
    points = np.array([-np.sqrt(0.6), 0.0, np.sqrt(0.6)])
    weights = np.array([5.0, 8.0, 5.0]) / 9.0

    def lagrange(at):
        values = np.ones(3)
        for j in range(3):
            for m in range(3):
                if m != j:
                    values[j] *= (at - points[m]) / (points[j] - points[m])
        return values

    derivative = np.zeros((3, 3))
    for i in range(3):
        for j in range(3):
            for k in range(3):
                if k != j:
                    term = 1.0 / (points[j] - points[k])
                    for m in range(3):
                        if m != j and m != k:
                            term *= (points[i] - points[m]) / (points[j] - points[m])
                    derivative[i, j] += term
    derivative[1, 1] = 0.0
    return derivative, (lagrange(-1.0), lagrange(1.0)), weights


DERIV, ENDS, WEIGHTS = line_tables()
SIGNS = (-1.0, 1.0)


def node(d, k, q):
    i, j = divmod(q, 3)
    at = [i, j]
    at.insert(d, k)
    return 9 * at[0] + 3 * at[1] + at[2]


def combine(coefficients, values):
    total = None
    for a, x in zip(coefficients, values):
        a = float(a)
        if a == 0.0:
            continue
        term = x if a == 1.0 else x * a
        total = term if total is None else total + term
    return total


def lanes(x, index):
    return jnp.take_along_axis(x, index, axis=1)


def kernel(
    n_dom,
    n_sub,
    lam_ref,
    visc_ref,
    vel_ref,
    inv_ref,
    part_ref,
    orient_ref,
    cnt_ref,
    dom_ref,
    sub_ref,
    out_ref,
    xs,
    vb,
    velb,
    invb,
    hmv,
    rate,
    tab,
    tp,
    jmp,
    nsum,
    grd,
    ehi,
    elo,
    ihi,
    ilo,
    rhi,
    rlo,
    ori,
    nat,
    dup,
    snear,
    ssub,
    sfar,
    rnear,
    rsub,
    rfar,
    send_sem,
    recv_sem,
):
    dom = lax.axis_index("dom")
    sub = lax.axis_index("sub")

    def at_dom(by):
        return (lax.rem(dom + by + n_dom, n_dom), sub)

    def has_dom(by):
        return dom + by >= 0 if by < 0 else dom + by < n_dom

    def at_sub(by):
        return (dom, lax.rem(sub + by + n_sub, n_sub))

    barrier = pltpu.get_barrier_semaphore()
    partners = 2
    for by in (-2, 2, -1, 1):
        partners = partners + jnp.where(has_dom(by), 1, 0)

        @pl.when(has_dom(by))
        def _(by=by):
            pl.semaphore_signal(barrier, inc=1, device_id=at_dom(by), device_id_type=MESH)

    for by in (-1, 1):
        pl.semaphore_signal(barrier, inc=1, device_id=at_sub(by), device_id_type=MESH)

    row = lax.broadcasted_iota(I32, (8, 128), 0)
    lane = lax.broadcasted_iota(I32, (8, 128), 1)
    low = row < 4
    half = jnp.where(low, 0, 1)
    left = lane < 64

    def spread(ref, r):
        return jnp.broadcast_to(ref[pl.ds(r, 1), :], (8, 128))

    def halves(ref, r, c):
        a = ref[pl.ds(r, 1), pl.ds(256 * c, 128)]
        b = ref[pl.ds(r, 1), pl.ds(256 * c + 128, 128)]
        return jnp.where(low, jnp.broadcast_to(a, (8, 128)), jnp.broadcast_to(b, (8, 128)))

    for c in range(2):
        for n in range(27):
            parts = [lam_ref[n, :, pl.ds(256 * c + 128 * h, 128)] for h in range(2)]
            xs[0, c, n] = jnp.concatenate(parts, axis=0)
        mean = None
        for n in range(27):
            v = halves(visc_ref, n, c)
            vb[c, n] = v
            w = float(WEIGHTS[n // 9] * WEIGHTS[n // 3 % 3] * WEIGHTS[n % 3])
            mean = v * w if mean is None else mean + v * w
        mean = mean * 0.125
        inv = halves(inv_ref, 0, c)
        invb[c] = inv
        hmv[c] = 0.5 * mean
        for d in range(3):
            speed = halves(vel_ref, d, c)
            velb[c, d] = speed
            for s in range(2):
                outward = speed if s == 0 else -speed
                rate[2 * (2 * d + s) + c] = jnp.minimum(outward, 0.0) + 2.0 * (mean * inv)

    def entries(k):
        if k < 4:
            a = dom_ref[pl.ds(1 + k // 2, 1), pl.ds(128 * (k % 2), 128)]
            return jnp.broadcast_to(a, (8, 128))
        if k < 6:
            return jnp.broadcast_to(sub_ref[pl.ds(k - 4, 1), :], (8, 128))
        a = jnp.broadcast_to(dom_ref[pl.ds(0, 1), pl.ds(0, 128)], (8, 128))
        b = jnp.broadcast_to(dom_ref[pl.ds(3, 1), pl.ds(0, 128)], (8, 128))
        return jnp.where(left, a, pltpu.roll(b, 64, 1))

    def valid(k):
        if k < 4:
            return lane + 128 * (k % 2) < cnt_ref[1 + k // 2]
        if k < 6:
            return lane >= 0
        return jnp.where(left, lane, lane - 64) < jnp.where(left, cnt_ref[0], cnt_ref[3])

    wide = lax.broadcasted_iota(I32, (128, 128), 0)
    found = jnp.zeros((48, 128), F32)
    for k in range(7):
        e = entries(k)
        hi = lax.shift_right_logical(e, 7)
        lo = lax.bitwise_and(e, 127)
        ehi[k] = hi
        elo[k] = lo
        ok = valid(k)
        where_row = [jnp.where((hi == row + 8 * b) & ok, 1.0, 0.0) for b in range(3)]
        lane_f = lane.astype(F32)
        left_rows = [x * float(k + 1) for x in where_row] + [x * lane_f for x in where_row]
        a = jnp.concatenate(left_rows, axis=0).astype(jnp.bfloat16)
        b = jnp.where(jnp.concatenate([lo] * 16, axis=0) == wide, 1.0, 0.0).astype(jnp.bfloat16)
        found = found + lax.dot_general(
            a, b, (((1,), (1,)), ((), ())), preferred_element_type=F32
        )
    nat[...] = found.astype(I32)

    for f in range(6):
        for c in range(2):
            g = 2 * f + c
            ra, rb = 4 * f + 2 * c, 4 * f + 2 * c + 1
            p = jnp.where(low, spread(part_ref, ra), spread(part_ref, rb))
            r = lax.shift_right_logical(p, 7)
            swap = lax.bitwise_xor(lax.bitwise_and(r, 1), half)
            ihi[g] = swap * 12 + lax.shift_right_logical(r, 1)
            ilo[g] = lax.bitwise_and(p, 127)
            rhi[g] = jnp.where(low, spread(nat, ra), spread(nat, rb))
            rlo[g] = jnp.where(low, spread(nat, 24 + ra), spread(nat, 24 + rb))
            ori[g] = jnp.where(low, spread(orient_ref, ra), spread(orient_ref, rb))

    pl.semaphore_wait(barrier, partners)

    def put_table(f, c, values):
        g = 2 * f + c
        swapped = [pltpu.roll(x, 4, 0) for x in values]
        for q in range(9):
            tab[g, q] = values[q]
            tab[12 + g, q] = swapped[q]
        for k in range(5):
            if k < 4:
                tp[4 * f + 2 * c, k] = jnp.where(low, values[2 * k], swapped[2 * k + 1])
                tp[4 * f + 2 * c + 1, k] = jnp.where(low, swapped[2 * k], values[2 * k + 1])
            else:
                tp[4 * f + 2 * c, k] = values[8]
                tp[4 * f + 2 * c + 1, k] = swapped[8]

    def copies(rnd):
        plan = [
            (sfar.at[rnd, 0], rfar.at[rnd, 1], "dom", -2),
            (sfar.at[rnd, 1], rfar.at[rnd, 0], "dom", 2),
        ]
        for part in range(2):
            piece = pl.ds(5 * part, 5)
            plan.append((snear.at[rnd, 0, piece], rnear.at[rnd, 1, piece], "dom", -1))
            plan.append((snear.at[rnd, 1, piece], rnear.at[rnd, 0, piece], "dom", 1))
        plan.append((ssub.at[rnd, 0], rsub.at[rnd, 1], "sub", -1))
        plan.append((ssub.at[rnd, 1], rsub.at[rnd, 0], "sub", 1))
        made = []
        for i, (src, dst, axis, by) in enumerate(plan):
            copy = pltpu.make_async_remote_copy(
                src_ref=src,
                dst_ref=dst,
                send_sem=send_sem.at[rnd, i],
                recv_sem=recv_sem.at[rnd, i],
                device_id=at_dom(by) if axis == "dom" else at_sub(by),
                device_id_type=MESH,
            )
            made.append((copy, axis, by))
        return made

    def start(entry):
        copy, axis, by = entry
        if axis == "sub":
            copy.start()
        else:
            pl.when(has_dom(by))(copy.start)

    def wait_in(entry):
        copy, axis, by = entry
        if axis == "sub":
            copy.wait_recv()
        else:
            pl.when(has_dom(-by))(copy.wait_recv)

    def wait_out(entry):
        copy, axis, by = entry
        if axis == "sub":
            copy.wait_send()
        else:
            pl.when(has_dom(by))(copy.wait_send)

    def collect(k):
        hi, lo = ehi[k], elo[k]
        total = [None] * 5
        for s in range(24):
            here = hi == s
            for m in range(5):
                x = lanes(tp[s, m], lo)
                total[m] = x if s == 0 else jnp.where(here, x, total[m])
        return total

    def send(rnd):
        out = copies(rnd)
        x = collect(6)
        for m in range(3):
            a = x[2 * m]
            if m < 2:
                b = x[2 * m + 1]
                sfar[rnd, 0, m] = jnp.where(left, a, pltpu.roll(b, 64, 1))
                sfar[rnd, 1, m] = jnp.where(left, pltpu.roll(a, 64, 1), b)
            else:
                sfar[rnd, 0, m] = a
                sfar[rnd, 1, m] = pltpu.roll(a, 64, 1)
        start(out[0])
        start(out[1])
        for part in range(2):
            for side in range(2):
                x = collect(2 * side + part)
                for m in range(5):
                    snear[rnd, side, 5 * part + m] = x[m]
                start(out[2 + 2 * part + side])
        for side in range(2):
            x = collect(4 + side)
            for m in range(5):
                ssub[rnd, side, m] = x[m]
            start(out[6 + side])

    def local(into):
        def groups(b, carry):
            for u in range(6):
                g = 6 * b + u
                hi, lo = ihi[g], ilo[g]
                total = [None] * 9
                for s in range(24):
                    here = hi == s
                    for q in range(9):
                        x = lanes(tab[s, q], lo)
                        total[q] = x if s == 0 else jnp.where(here, x, total[q])
                for q in range(9):
                    into[g, q] = total[q]
            return carry

        lax.fori_loop(0, 2, groups, 0)

    def double(k, words):
        for m in range(5):
            x = words[m]
            y = pltpu.roll(x, 4, 0)
            dup[k, 2 * m] = jnp.where(low, x, y)
            if m < 4:
                dup[k, 2 * m + 1] = jnp.where(low, y, x)

    def merged(total, g, lists):
        hi, lo = rhi[g], rlo[g]
        for k in lists:
            here = hi == k + 1
            for q in range(9):
                total[q] = jnp.where(here, lanes(dup[k, q], lo), total[q])
        return total

    def arrive(rnd, into, difference):
        moved = copies(rnd)
        for entry in moved[6:]:
            wait_in(entry)
        for k in range(2):
            double(4 + k, [rsub[rnd, k, m] for m in range(5)])
        for entry in moved[2:6]:
            wait_in(entry)
        for k in range(4):
            double(k, [rnear[rnd, k // 2, 5 * (k % 2) + m] for m in range(5)])

        def first(b, carry):
            for u in range(6):
                g = 6 * b + u
                total = merged([into[g, q] for q in range(9)], g, range(6))
                for q in range(9):
                    into[g, q] = total[q]
            return carry

        lax.fori_loop(0, 2, first, 0)
        for entry in moved[:2]:
            wait_in(entry)
        far = []
        for m in range(3):
            a, b = rfar[rnd, 0, m], rfar[rnd, 1, m]
            far.append(jnp.where(left, a, pltpu.roll(b, 64, 1)))
            if m < 2:
                far.append(jnp.where(left, pltpu.roll(a, 64, 1), b))
        double(6, far)

        def last(b, carry):
            for u in range(6):
                g = 6 * b + u
                code = ori[g]
                total = merged([into[g, q] for q in range(9)], g, [6])
                flip_i = lax.bitwise_and(code, 1) == 1
                flip_j = lax.bitwise_and(code, 2) == 2
                swap = lax.bitwise_and(code, 4) == 4
                for j in range(3):
                    x, y = total[j], total[6 + j]
                    total[j] = jnp.where(flip_i, y, x)
                    total[6 + j] = jnp.where(flip_i, x, y)
                for i in range(3):
                    x, y = total[3 * i], total[3 * i + 2]
                    total[3 * i] = jnp.where(flip_j, y, x)
                    total[3 * i + 2] = jnp.where(flip_j, x, y)
                for i in range(3):
                    for j in range(i):
                        x, y = total[3 * i + j], total[3 * j + i]
                        total[3 * i + j] = jnp.where(swap, y, x)
                        total[3 * j + i] = jnp.where(swap, x, y)
                for q in range(9):
                    own = tab[g, q]
                    into[g, q] = total[q] - own if difference else total[q] + own
            return carry

        lax.fori_loop(0, 2, last, 0)

    def segment(seg, carry):
        def traces(c, carry):
            for d in range(3):
                face = ([], [])
                for q in range(9):
                    x = [xs[seg, c, node(d, k, q)] for k in range(3)]
                    for s in range(2):
                        face[s].append(combine(ENDS[s], x))
                for s in range(2):
                    put_table(2 * d + s, c, face[s])
            return carry

        lax.fori_loop(0, 2, traces, 0)
        send(2 * seg)
        local(jmp)
        arrive(2 * seg, jmp, True)

        def gradients(c, carry):
            inv = invb[c]
            for d in range(3):
                face = ([], [])
                for q in range(9):
                    x = [xs[seg, c, node(d, k, q)] for k in range(3)]
                    jumps = [jmp[2 * (2 * d + s) + c, q] for s in range(2)]
                    g = []
                    for k in range(3):
                        lift = [0.5 * SIGNS[s] * ENDS[s][k] / WEIGHTS[k] for s in range(2)]
                        g.append(inv * combine(list(DERIV[k]) + lift, x + jumps))
                        grd[c, d, 3 * q + k] = g[k]
                    for s in range(2):
                        face[s].append(combine(SIGNS[s] * ENDS[s], g))
                for s in range(2):
                    put_table(2 * d + s, c, face[s])
            return carry

        lax.fori_loop(0, 2, gradients, 0)
        send(2 * seg + 1)
        local(nsum)
        arrive(2 * seg + 1, nsum, False)

        def advance(c):
            inv, drag = invb[c], hmv[c]
            total = [None] * 27
            for d in range(3):
                speed = velb[c, d]
                rates = [rate[2 * (2 * d + s) + c] for s in range(2)]
                for q in range(9):
                    flux = []
                    for k in range(3):
                        n = node(d, k, q)
                        flux.append(vb[c, n] * grd[c, d, 3 * q + k] - speed * xs[seg, c, n])
                    surface = []
                    for s in range(2):
                        g = 2 * (2 * d + s) + c
                        surface.append(rates[s] * jmp[g, q] - drag * nsum[g, q])
                    for k in range(3):
                        n = node(d, k, q)
                        lift = [ENDS[s][k] / WEIGHTS[k] for s in range(2)]
                        term = combine(list(DERIV[k]) + lift, flux + surface)
                        total[n] = term if total[n] is None else total[n] + term
            scale = STEP * inv
            for n in range(27):
                new = xs[seg, c, n] + scale * total[n]
                xs[seg + 1, c, n] = new
                result = 0.5 * (xs[0, c, n] + new)
                for h in range(2):
                    out_ref[n, :, pl.ds(256 * c + 128 * h, 128)] = result[4 * h : 4 * h + 4]

        advance(0)
        advance(1)
        return carry

    lax.fori_loop(0, 2, segment, 0)

    def drain(rnd, carry):
        for entry in copies(rnd):
            wait_out(entry)
        return carry

    lax.fori_loop(0, 4, drain, 0)


def on_device(
    n_dom,
    n_sub,
    adjoint_in,
    viscosity,
    velocity,
    inverse_size,
    local_partner,
    face_orient,
    dom_counts,
    dom_slots,
    sub_slots,
):
    lam = adjoint_in.transpose(1, 0, 2)
    vmem = pl.BlockSpec(memory_space=pltpu.VMEM)
    smem = pl.BlockSpec(memory_space=pltpu.SMEM)
    tile = (8, 128)
    out = pl.pallas_call(
        functools.partial(kernel, n_dom, n_sub),
        out_shape=jax.ShapeDtypeStruct((27, 4, 512), F32),
        in_specs=[vmem] * 6 + [smem] + [vmem] * 2,
        out_specs=vmem,
        scratch_shapes=[
            pltpu.VMEM((3, 2, 27) + tile, F32),
            pltpu.VMEM((2, 27) + tile, F32),
            pltpu.VMEM((2, 3) + tile, F32),
            pltpu.VMEM((2,) + tile, F32),
            pltpu.VMEM((2,) + tile, F32),
            pltpu.VMEM((12,) + tile, F32),
            pltpu.VMEM((24, 9) + tile, F32),
            pltpu.VMEM((24, 5) + tile, F32),
            pltpu.VMEM((12, 9) + tile, F32),
            pltpu.VMEM((12, 9) + tile, F32),
            pltpu.VMEM((2, 3, 27) + tile, F32),
            pltpu.VMEM((7,) + tile, I32),
            pltpu.VMEM((7,) + tile, I32),
            pltpu.VMEM((12,) + tile, I32),
            pltpu.VMEM((12,) + tile, I32),
            pltpu.VMEM((12,) + tile, I32),
            pltpu.VMEM((12,) + tile, I32),
            pltpu.VMEM((12,) + tile, I32),
            pltpu.VMEM((48, 128), I32),
            pltpu.VMEM((7, 9) + tile, F32),
            pltpu.VMEM((4, 2, 10) + tile, F32),
            pltpu.VMEM((4, 2, 5) + tile, F32),
            pltpu.VMEM((4, 2, 3) + tile, F32),
            pltpu.VMEM((4, 2, 10) + tile, F32),
            pltpu.VMEM((4, 2, 5) + tile, F32),
            pltpu.VMEM((4, 2, 3) + tile, F32),
            pltpu.SemaphoreType.DMA((4, 8)),
            pltpu.SemaphoreType.DMA((4, 8)),
        ],
        compiler_params=pltpu.CompilerParams(collective_id=0, has_side_effects=True),
        name="segments",
    )(
        lam,
        viscosity,
        velocity,
        inverse_size.reshape(1, 512),
        local_partner.reshape(24, 128),
        face_orient.reshape(24, 128),
        dom_counts.reshape(4),
        dom_slots.reshape(4, 256),
        sub_slots.reshape(2, 128),
    )
    return out.transpose(1, 0, 2)


def solution(mesh):
    in_specs = (
        P(None, None, ("dom", "sub")),
        P(None, ("dom", "sub")),
        P(None, ("dom", "sub")),
        P(("dom", "sub")),
        P("dom", "sub", None),
        P("dom", "sub", None),
        P("dom", "sub", None),
        P("dom", "sub", None, None),
        P("dom", "sub", None, None),
    )
    return jax.shard_map(
        functools.partial(on_device, mesh.shape["dom"], mesh.shape["sub"]),
        mesh=mesh,
        in_specs=in_specs,
        out_specs=P(None, None, ("dom", "sub")),
        check_vma=False,
    )
```

```python
import functools

import jax
import jax.numpy as jnp
import numpy as np
from jax import lax
from jax.experimental import pallas as pl
from jax.experimental.pallas import tpu as pltpu
from jax.sharding import PartitionSpec as P

MESH = pl.DeviceIdType.MESH
STEP = 0.02
F32 = jnp.float32
I32 = jnp.int32


def line_tables():
    points = np.array([-np.sqrt(0.6), 0.0, np.sqrt(0.6)])
    weights = np.array([5.0, 8.0, 5.0]) / 9.0

    def lagrange(at):
        values = np.ones(3)
        for j in range(3):
            for m in range(3):
                if m != j:
                    values[j] *= (at - points[m]) / (points[j] - points[m])
        return values

    derivative = np.zeros((3, 3))
    for i in range(3):
        for j in range(3):
            for k in range(3):
                if k != j:
                    term = 1.0 / (points[j] - points[k])
                    for m in range(3):
                        if m != j and m != k:
                            term *= (points[i] - points[m]) / (points[j] - points[m])
                    derivative[i, j] += term
    derivative[1, 1] = 0.0
    return derivative, (lagrange(-1.0), lagrange(1.0)), weights


DERIV, ENDS, WEIGHTS = line_tables()
SIGNS = (-1.0, 1.0)


def node(d, k, q):
    i, j = divmod(q, 3)
    at = [i, j]
    at.insert(d, k)
    return 9 * at[0] + 3 * at[1] + at[2]


def combine(coefficients, values):
    total = None
    for a, x in zip(coefficients, values):
        a = float(a)
        if a == 0.0:
            continue
        term = x if a == 1.0 else x * a
        total = term if total is None else total + term
    return total


def lanes(x, index):
    return jnp.take_along_axis(x, index, axis=1)


def kernel(
    n_dom,
    n_sub,
    lam_in,
    visc_in,
    vel_in,
    inv_in,
    part_in,
    orient_in,
    cnt_in,
    dom_in,
    sub_in,
    out_ref,
    lam_ref,
    visc_ref,
    vel_ref,
    inv_ref,
    part_ref,
    orient_ref,
    cnt_ref,
    dom_ref,
    sub_ref,
    in_sem,
    xs,
    vb,
    velb,
    invb,
    hmv,
    rate,
    tab,
    tp,
    jmp,
    nsum,
    grd,
    ehi,
    elo,
    ihi,
    ilo,
    rhi,
    rlo,
    ori,
    nat,
    dup,
    picks,
    split,
    snear,
    ssub,
    sfar,
    rnear,
    rsub,
    rfar,
    send_sem,
    recv_sem,
):
    dom = lax.axis_index("dom")
    sub = lax.axis_index("sub")

    def at_dom(by):
        return (lax.rem(dom + by + n_dom, n_dom), sub)

    def has_dom(by):
        return dom + by >= 0 if by < 0 else dom + by < n_dom

    def at_sub(by):
        return (dom, lax.rem(sub + by + n_sub, n_sub))

    arrays = (
        (lam_in, lam_ref),
        (dom_in, dom_ref),
        (sub_in, sub_ref),
        (cnt_in, cnt_ref),
        (part_in, part_ref),
        (orient_in, orient_ref),
        (visc_in, visc_ref),
        (vel_in, vel_ref),
        (inv_in, inv_ref),
    )
    loads = [
        pltpu.make_async_copy(src, dst, in_sem.at[i]) for i, (src, dst) in enumerate(arrays)
    ]
    for load in loads:
        load.start()

    barrier = pltpu.get_barrier_semaphore()
    partners = 2
    for by in (-2, 2, -1, 1):
        partners = partners + jnp.where(has_dom(by), 1, 0)

        @pl.when(has_dom(by))
        def _(by=by):
            pl.semaphore_signal(barrier, inc=1, device_id=at_dom(by), device_id_type=MESH)

    for by in (-1, 1):
        pl.semaphore_signal(barrier, inc=1, device_id=at_sub(by), device_id_type=MESH)

    row = lax.broadcasted_iota(I32, (8, 128), 0)
    lane = lax.broadcasted_iota(I32, (8, 128), 1)
    low = row < 4
    half = jnp.where(low, 0, 1)
    left = lane < 64

    def spread(ref, r):
        return jnp.broadcast_to(ref[pl.ds(r, 1), :], (8, 128))

    def halves(ref, r, c):
        a = ref[pl.ds(r, 1), pl.ds(256 * c, 128)]
        b = ref[pl.ds(r, 1), pl.ds(256 * c + 128, 128)]
        return jnp.where(low, jnp.broadcast_to(a, (8, 128)), jnp.broadcast_to(b, (8, 128)))

    def entries(k):
        if k < 4:
            a = dom_ref[pl.ds(1 + k // 2, 1), pl.ds(128 * (k % 2), 128)]
            return jnp.broadcast_to(a, (8, 128))
        if k < 6:
            return jnp.broadcast_to(sub_ref[pl.ds(k - 4, 1), :], (8, 128))
        a = jnp.broadcast_to(dom_ref[pl.ds(0, 1), pl.ds(0, 128)], (8, 128))
        b = jnp.broadcast_to(dom_ref[pl.ds(3, 1), pl.ds(0, 128)], (8, 128))
        return jnp.where(left, a, pltpu.roll(b, 64, 1))

    def valid(k):
        if k < 4:
            return lane + 128 * (k % 2) < cnt_ref[1 + k // 2]
        if k < 6:
            return lane >= 0
        return jnp.where(left, lane, lane - 64) < jnp.where(left, cnt_ref[0], cnt_ref[3])

    for load in loads[:3]:
        load.wait()
    for k in range(7):
        e = entries(k)
        ehi[k] = lax.shift_right_logical(e, 7)
        elo[k] = lax.bitwise_and(e, 127)
    for c in range(2):
        for n in range(27):
            parts = [lam_ref[n, :, pl.ds(256 * c + 128 * h, 128)] for h in range(2)]
            xs[0, c, n] = jnp.concatenate(parts, axis=0)

    def prepare():
        for load in loads[3:]:
            load.wait()
        for c in range(2):
            mean = None
            for n in range(27):
                v = halves(visc_ref, n, c)
                vb[c, n] = v
                w = float(WEIGHTS[n // 9] * WEIGHTS[n // 3 % 3] * WEIGHTS[n % 3])
                mean = v * w if mean is None else mean + v * w
            mean = mean * 0.125
            inv = halves(inv_ref, 0, c)
            invb[c] = inv
            hmv[c] = 0.5 * mean
            for d in range(3):
                speed = halves(vel_ref, d, c)
                velb[c, d] = speed
                for s in range(2):
                    outward = speed if s == 0 else -speed
                    rate[2 * (2 * d + s) + c] = jnp.minimum(outward, 0.0) + 2.0 * (mean * inv)

        wide = lax.broadcasted_iota(I32, (128, 128), 0)
        found = jnp.zeros((48, 128), F32)
        for k in range(7):
            e = entries(k)
            hi = lax.shift_right_logical(e, 7)
            lo = lax.bitwise_and(e, 127)
            ok = valid(k)
            where_row = [jnp.where((hi == row + 8 * b) & ok, 1.0, 0.0) for b in range(3)]
            lane_f = lane.astype(F32)
            left_rows = [x * float(k + 1) for x in where_row] + [x * lane_f for x in where_row]
            a = jnp.concatenate(left_rows, axis=0).astype(jnp.bfloat16)
            b = jnp.where(jnp.concatenate([lo] * 16, axis=0) == wide, 1.0, 0.0).astype(jnp.bfloat16)
            found = found + lax.dot_general(
                a, b, (((1,), (1,)), ((), ())), preferred_element_type=F32
            )
        nat[...] = found.astype(I32)

        for f in range(6):
            for c in range(2):
                g = 2 * f + c
                ra, rb = 4 * f + 2 * c, 4 * f + 2 * c + 1
                p = jnp.where(low, spread(part_ref, ra), spread(part_ref, rb))
                r = lax.shift_right_logical(p, 7)
                swap = lax.bitwise_xor(lax.bitwise_and(r, 1), half)
                ihi[g] = swap * 12 + lax.shift_right_logical(r, 1)
                ilo[g] = lax.bitwise_and(p, 127)
                rhi[g] = jnp.where(low, spread(nat, ra), spread(nat, rb))
                rlo[g] = jnp.where(low, spread(nat, 24 + ra), spread(nat, 24 + rb))
                ori[g] = jnp.where(low, spread(orient_ref, ra), spread(orient_ref, rb))

    def put_table(f, c, values):
        g = 2 * f + c
        swapped = [pltpu.roll(x, 4, 0) for x in values]
        for q in range(9):
            tab[g, q] = values[q]
            tab[12 + g, q] = swapped[q]
        for k in range(5):
            if k < 4:
                tp[4 * f + 2 * c, k] = jnp.where(low, values[2 * k], swapped[2 * k + 1])
                tp[4 * f + 2 * c + 1, k] = jnp.where(low, swapped[2 * k], values[2 * k + 1])
            else:
                tp[4 * f + 2 * c, k] = values[8]
                tp[4 * f + 2 * c + 1, k] = swapped[8]

    def copies(rnd):
        plan = [
            (sfar.at[rnd, 0], rfar.at[rnd, 1], "dom", -2),
            (sfar.at[rnd, 1], rfar.at[rnd, 0], "dom", 2),
        ]
        for part in range(2):
            piece = pl.ds(5 * part, 5)
            plan.append((snear.at[rnd, 0, piece], rnear.at[rnd, 1, piece], "dom", -1))
            plan.append((snear.at[rnd, 1, piece], rnear.at[rnd, 0, piece], "dom", 1))
        plan.append((ssub.at[rnd, 0], rsub.at[rnd, 1], "sub", -1))
        plan.append((ssub.at[rnd, 1], rsub.at[rnd, 0], "sub", 1))
        made = []
        for i, (src, dst, axis, by) in enumerate(plan):
            copy = pltpu.make_async_remote_copy(
                src_ref=src,
                dst_ref=dst,
                send_sem=send_sem.at[rnd, i],
                recv_sem=recv_sem.at[rnd, i],
                device_id=at_dom(by) if axis == "dom" else at_sub(by),
                device_id_type=MESH,
            )
            made.append((copy, axis, by))
        return made

    def start(entry):
        copy, axis, by = entry
        if axis == "sub":
            copy.start()
        else:
            pl.when(has_dom(by))(copy.start)

    def wait_in(entry):
        copy, axis, by = entry
        if axis == "sub":
            copy.wait_recv()
        else:
            pl.when(has_dom(-by))(copy.wait_recv)

    def wait_out(entry):
        copy, axis, by = entry
        if axis == "sub":
            copy.wait_send()
        else:
            pl.when(has_dom(by))(copy.wait_send)

    def collect(k):
        hi, lo = ehi[k], elo[k]
        total = [None] * 5
        for s in range(24):
            here = hi == s
            for m in range(5):
                x = lanes(tp[s, m], lo)
                total[m] = x if s == 0 else jnp.where(here, x, total[m])
        return total

    def send(rnd):
        out = copies(rnd)
        x = collect(6)
        for m in range(3):
            a = x[2 * m]
            if m < 2:
                b = x[2 * m + 1]
                sfar[rnd, 0, m] = jnp.where(left, a, pltpu.roll(b, 64, 1))
                sfar[rnd, 1, m] = jnp.where(left, pltpu.roll(a, 64, 1), b)
            else:
                sfar[rnd, 0, m] = a
                sfar[rnd, 1, m] = pltpu.roll(a, 64, 1)

        @pl.when(rnd == 0)
        def _():
            pl.semaphore_wait(barrier, partners)

        start(out[0])
        start(out[1])
        for part in range(2):
            for side in range(2):
                x = collect(2 * side + part)
                for m in range(5):
                    snear[rnd, side, 5 * part + m] = x[m]
                start(out[2 + 2 * part + side])
        for side in range(2):
            x = collect(4 + side)
            for m in range(5):
                ssub[rnd, side, m] = x[m]
            start(out[6 + side])

    def gathered(g):
        hi, lo = ihi[g], ilo[g]
        total = [None] * 9
        for s in range(24):
            here = hi == s
            for q in range(9):
                x = lanes(tab[s, q], lo)
                total[q] = x if s == 0 else jnp.where(here, x, total[q])
        return total

    def local_first(into):
        depth = lax.broadcasted_iota(I32, (128, 128), 0).astype(jnp.int16)

        def groups(b, carry):
            for u in range(6):
                g = 6 * b + u
                total = gathered(g)
                for q in range(9):
                    into[g, q] = total[q]
            for u in range(2):
                j = 2 * b + u
                wanted = jnp.broadcast_to(part_ref[pl.ds(20 + j, 1), :], (128, 128))
                wanted = wanted.astype(jnp.int16)
                one = jnp.ones((128, 128), jnp.bfloat16)
                zero = jnp.zeros((128, 128), jnp.bfloat16)
                for i in range(24):
                    place = wanted == depth + jnp.int16(128 * i)
                    picks[b, pl.ds(128 * i, 128), pl.ds(128 * u, 128)] = jnp.where(
                        place, one, zero
                    )
            return carry

        lax.fori_loop(0, 2, groups, 0)

    def local_later(into):
        zero = jnp.zeros((8, 128), F32)
        for r in range(24):
            words = [tp[r, m] for m in range(5)] + [zero]
            for m in range(3):
                x = jnp.concatenate(words[2 * m : 2 * m + 2], axis=0)
                high = x.astype(jnp.bfloat16)
                rest = (x - high.astype(F32)).astype(jnp.bfloat16)
                split[pl.ds(16 * m, 16), pl.ds(128 * r, 128)] = high
                split[pl.ds(48 + 16 * m, 16), pl.ds(128 * r, 128)] = rest
        for c in range(2):
            for u in range(5):
                g = 5 * c + u
                total = gathered(g)
                for q in range(9):
                    into[g, q] = total[q]
            both = jnp.dot(split[...], picks[c], preferred_element_type=F32)
            value = both[:48] + both[48:]
            g = 10 + c
            for m in range(5):
                x, y = [value[8 * m : 8 * m + 8, 128 * h : 128 * h + 128] for h in range(2)]
                into[g, 2 * m] = jnp.where(low, x, pltpu.roll(y, 4, 0))
                if m < 4:
                    into[g, 2 * m + 1] = jnp.where(low, pltpu.roll(x, 4, 0), y)

    def double(k, words):
        for m in range(5):
            x = words[m]
            y = pltpu.roll(x, 4, 0)
            dup[k, 2 * m] = jnp.where(low, x, y)
            if m < 4:
                dup[k, 2 * m + 1] = jnp.where(low, y, x)

    def merged(total, g, lists):
        hi, lo = rhi[g], rlo[g]
        for k in lists:
            here = hi == k + 1
            for q in range(9):
                total[q] = jnp.where(here, lanes(dup[k, q], lo), total[q])
        return total

    def arrive(rnd, into, difference):
        moved = copies(rnd)
        for entry in moved[6:]:
            wait_in(entry)
        for k in range(2):
            double(4 + k, [rsub[rnd, k, m] for m in range(5)])

        def merge(lists):
            for g in range(12):
                total = merged([into[g, q] for q in range(9)], g, lists)
                for q in range(9):
                    into[g, q] = total[q]

        merge([4, 5])
        for entry in moved[2:4]:
            wait_in(entry)
        for k in (0, 2):
            double(k, [rnear[rnd, k // 2, m] for m in range(5)])
        merge([0, 2])
        for entry in moved[4:6] + moved[:2]:
            wait_in(entry)
        for k in (1, 3):
            double(k, [rnear[rnd, k // 2, 5 + m] for m in range(5)])
        far = []
        for m in range(3):
            a, b = rfar[rnd, 0, m], rfar[rnd, 1, m]
            far.append(jnp.where(left, a, pltpu.roll(b, 64, 1)))
            if m < 2:
                far.append(jnp.where(left, pltpu.roll(a, 64, 1), b))
        double(6, far)

        def last(b, carry):
            for u in range(6):
                g = 6 * b + u
                code = ori[g]
                total = merged([into[g, q] for q in range(9)], g, [1, 3, 6])
                flip_i = lax.bitwise_and(code, 1) == 1
                flip_j = lax.bitwise_and(code, 2) == 2
                swap = lax.bitwise_and(code, 4) == 4
                for j in range(3):
                    x, y = total[j], total[6 + j]
                    total[j] = jnp.where(flip_i, y, x)
                    total[6 + j] = jnp.where(flip_i, x, y)
                for i in range(3):
                    x, y = total[3 * i], total[3 * i + 2]
                    total[3 * i] = jnp.where(flip_j, y, x)
                    total[3 * i + 2] = jnp.where(flip_j, x, y)
                for i in range(3):
                    for j in range(i):
                        x, y = total[3 * i + j], total[3 * j + i]
                        total[3 * i + j] = jnp.where(swap, y, x)
                        total[3 * j + i] = jnp.where(swap, x, y)
                for q in range(9):
                    own = tab[g, q]
                    into[g, q] = total[q] - own if difference else total[q] + own
            return carry

        lax.fori_loop(0, 2, last, 0)

    def segment(seg, carry):
        def traces(c, carry):
            for d in range(3):
                face = ([], [])
                for q in range(9):
                    x = [xs[seg, c, node(d, k, q)] for k in range(3)]
                    for s in range(2):
                        face[s].append(combine(ENDS[s], x))
                for s in range(2):
                    put_table(2 * d + s, c, face[s])
            return carry

        lax.fori_loop(0, 2, traces, 0)
        send(2 * seg)
        pl.when(seg == 0)(prepare)
        pl.when(seg == 0)(functools.partial(local_first, jmp))
        pl.when(seg != 0)(functools.partial(local_later, jmp))
        arrive(2 * seg, jmp, True)

        def gradients(c, carry):
            inv = invb[c]
            for d in range(3):
                face = ([], [])
                for q in range(9):
                    x = [xs[seg, c, node(d, k, q)] for k in range(3)]
                    jumps = [jmp[2 * (2 * d + s) + c, q] for s in range(2)]
                    g = []
                    for k in range(3):
                        lift = [0.5 * SIGNS[s] * ENDS[s][k] / WEIGHTS[k] for s in range(2)]
                        g.append(inv * combine(list(DERIV[k]) + lift, x + jumps))
                        grd[c, d, 3 * q + k] = g[k]
                    for s in range(2):
                        face[s].append(combine(SIGNS[s] * ENDS[s], g))
                for s in range(2):
                    put_table(2 * d + s, c, face[s])
            return carry

        lax.fori_loop(0, 2, gradients, 0)
        send(2 * seg + 1)
        local_later(nsum)
        arrive(2 * seg + 1, nsum, False)

        def advance(c):
            inv, drag = invb[c], hmv[c]
            total = [None] * 27
            for d in range(3):
                speed = velb[c, d]
                rates = [rate[2 * (2 * d + s) + c] for s in range(2)]
                for q in range(9):
                    flux = []
                    for k in range(3):
                        n = node(d, k, q)
                        flux.append(vb[c, n] * grd[c, d, 3 * q + k] - speed * xs[seg, c, n])
                    surface = []
                    for s in range(2):
                        g = 2 * (2 * d + s) + c
                        surface.append(rates[s] * jmp[g, q] - drag * nsum[g, q])
                    for k in range(3):
                        n = node(d, k, q)
                        lift = [ENDS[s][k] / WEIGHTS[k] for s in range(2)]
                        term = combine(list(DERIV[k]) + lift, flux + surface)
                        total[n] = term if total[n] is None else total[n] + term
            scale = STEP * inv
            for n in range(27):
                new = xs[seg, c, n] + scale * total[n]
                xs[seg + 1, c, n] = new
                result = 0.5 * (xs[0, c, n] + new)
                for h in range(2):
                    out_ref[n, :, pl.ds(256 * c + 128 * h, 128)] = result[4 * h : 4 * h + 4]

        advance(0)
        advance(1)
        return carry

    lax.fori_loop(0, 2, segment, 0)

    def drain(rnd, carry):
        for entry in copies(rnd):
            wait_out(entry)
        return carry

    lax.fori_loop(0, 4, drain, 0)


def on_device(
    n_dom,
    n_sub,
    adjoint_in,
    viscosity,
    velocity,
    inverse_size,
    local_partner,
    face_orient,
    dom_counts,
    dom_slots,
    sub_slots,
):
    lam = adjoint_in.transpose(1, 0, 2)
    vmem = pl.BlockSpec(memory_space=pltpu.VMEM)
    tile = (8, 128)
    out = pl.pallas_call(
        functools.partial(kernel, n_dom, n_sub),
        out_shape=jax.ShapeDtypeStruct((27, 4, 512), F32),
        in_specs=[pl.BlockSpec(memory_space=pl.ANY)] * 9,
        out_specs=vmem,
        scratch_shapes=[
            pltpu.VMEM((27, 4, 512), F32),
            pltpu.VMEM((27, 512), F32),
            pltpu.VMEM((3, 512), F32),
            pltpu.VMEM((1, 512), F32),
            pltpu.VMEM((24, 128), I32),
            pltpu.VMEM((24, 128), I32),
            pltpu.SMEM((4,), I32),
            pltpu.VMEM((4, 256), I32),
            pltpu.VMEM((2, 128), I32),
            pltpu.SemaphoreType.DMA((9,)),
            pltpu.VMEM((3, 2, 27) + tile, F32),
            pltpu.VMEM((2, 27) + tile, F32),
            pltpu.VMEM((2, 3) + tile, F32),
            pltpu.VMEM((2,) + tile, F32),
            pltpu.VMEM((2,) + tile, F32),
            pltpu.VMEM((12,) + tile, F32),
            pltpu.VMEM((24, 9) + tile, F32),
            pltpu.VMEM((24, 5) + tile, F32),
            pltpu.VMEM((12, 9) + tile, F32),
            pltpu.VMEM((12, 9) + tile, F32),
            pltpu.VMEM((2, 3, 27) + tile, F32),
            pltpu.VMEM((7,) + tile, I32),
            pltpu.VMEM((7,) + tile, I32),
            pltpu.VMEM((12,) + tile, I32),
            pltpu.VMEM((12,) + tile, I32),
            pltpu.VMEM((12,) + tile, I32),
            pltpu.VMEM((12,) + tile, I32),
            pltpu.VMEM((12,) + tile, I32),
            pltpu.VMEM((48, 128), I32),
            pltpu.VMEM((7, 9) + tile, F32),
            pltpu.VMEM((2, 3072, 256), jnp.bfloat16),
            pltpu.VMEM((96, 3072), jnp.bfloat16),
            pltpu.VMEM((4, 2, 10) + tile, F32),
            pltpu.VMEM((4, 2, 5) + tile, F32),
            pltpu.VMEM((4, 2, 3) + tile, F32),
            pltpu.VMEM((4, 2, 10) + tile, F32),
            pltpu.VMEM((4, 2, 5) + tile, F32),
            pltpu.VMEM((4, 2, 3) + tile, F32),
            pltpu.SemaphoreType.DMA((4, 8)),
            pltpu.SemaphoreType.DMA((4, 8)),
        ],
        compiler_params=pltpu.CompilerParams(collective_id=0, has_side_effects=True),
        name="segments",
    )(
        lam,
        viscosity,
        velocity,
        inverse_size.reshape(1, 512),
        local_partner.reshape(24, 128),
        face_orient.reshape(24, 128),
        dom_counts.reshape(4),
        dom_slots.reshape(4, 256),
        sub_slots.reshape(2, 128),
    )
    return out.transpose(1, 0, 2)


def solution(mesh):
    in_specs = (
        P(None, None, ("dom", "sub")),
        P(None, ("dom", "sub")),
        P(None, ("dom", "sub")),
        P(("dom", "sub")),
        P("dom", "sub", None),
        P("dom", "sub", None),
        P("dom", "sub", None),
        P("dom", "sub", None, None),
        P("dom", "sub", None, None),
    )
    return jax.shard_map(
        functools.partial(on_device, mesh.shape["dom"], mesh.shape["sub"]),
        mesh=mesh,
        in_specs=in_specs,
        out_specs=P(None, None, ("dom", "sub")),
        check_vma=False,
    )
```

```python
import functools

import jax
import jax.numpy as jnp
import numpy as np
from jax import lax
from jax.experimental import pallas as pl
from jax.experimental.pallas import tpu as pltpu
from jax.sharding import PartitionSpec as P

MESH = pl.DeviceIdType.MESH
STEP = 0.02
F32 = jnp.float32
I32 = jnp.int32


def line_tables():
    points = np.array([-np.sqrt(0.6), 0.0, np.sqrt(0.6)])
    weights = np.array([5.0, 8.0, 5.0]) / 9.0

    def lagrange(at):
        values = np.ones(3)
        for j in range(3):
            for m in range(3):
                if m != j:
                    values[j] *= (at - points[m]) / (points[j] - points[m])
        return values

    derivative = np.zeros((3, 3))
    for i in range(3):
        for j in range(3):
            for k in range(3):
                if k != j:
                    term = 1.0 / (points[j] - points[k])
                    for m in range(3):
                        if m != j and m != k:
                            term *= (points[i] - points[m]) / (points[j] - points[m])
                    derivative[i, j] += term
    derivative[1, 1] = 0.0
    return derivative, (lagrange(-1.0), lagrange(1.0)), weights


DERIV, ENDS, WEIGHTS = line_tables()
SIGNS = (-1.0, 1.0)


def node(d, k, q):
    i, j = divmod(q, 3)
    at = [i, j]
    at.insert(d, k)
    return 9 * at[0] + 3 * at[1] + at[2]


def combine(coefficients, values):
    total = None
    for a, x in zip(coefficients, values):
        a = float(a)
        if a == 0.0:
            continue
        term = x if a == 1.0 else x * a
        total = term if total is None else total + term
    return total


def lanes(x, index):
    return jnp.take_along_axis(x, index, axis=1)


def kernel(
    n_dom,
    n_sub,
    lam_in,
    visc_in,
    vel_in,
    inv_in,
    part_in,
    orient_in,
    cnt_in,
    dom_in,
    sub_in,
    out_ref,
    lam_ref,
    visc_ref,
    vel_ref,
    inv_ref,
    part_ref,
    orient_ref,
    cnt_ref,
    dom_ref,
    sub_ref,
    in_sem,
    xs,
    vb,
    velb,
    invb,
    hmv,
    rate,
    tab,
    tp,
    jmp,
    nsum,
    grd,
    ehi,
    elo,
    ihi,
    ilo,
    rhi,
    rlo,
    ori,
    nat,
    dup,
    picks,
    split,
    snear,
    ssub,
    sfar,
    rnear,
    rsub,
    rfar,
    send_sem,
    recv_sem,
):
    dom = lax.axis_index("dom")
    sub = lax.axis_index("sub")

    def at_dom(by):
        return (lax.rem(dom + by + n_dom, n_dom), sub)

    def has_dom(by):
        return dom + by >= 0 if by < 0 else dom + by < n_dom

    def at_sub(by):
        return (dom, lax.rem(sub + by + n_sub, n_sub))

    arrays = (
        (lam_in, lam_ref),
        (dom_in, dom_ref),
        (sub_in, sub_ref),
        (cnt_in, cnt_ref),
        (part_in, part_ref),
        (orient_in, orient_ref),
        (visc_in, visc_ref),
        (vel_in, vel_ref),
        (inv_in, inv_ref),
    )
    loads = [
        pltpu.make_async_copy(src, dst, in_sem.at[i]) for i, (src, dst) in enumerate(arrays)
    ]
    for load in loads:
        load.start()

    barrier = pltpu.get_barrier_semaphore()
    partners = 2
    for by in (-2, 2, -1, 1):
        partners = partners + jnp.where(has_dom(by), 1, 0)

        @pl.when(has_dom(by))
        def _(by=by):
            pl.semaphore_signal(barrier, inc=1, device_id=at_dom(by), device_id_type=MESH)

    for by in (-1, 1):
        pl.semaphore_signal(barrier, inc=1, device_id=at_sub(by), device_id_type=MESH)

    row = lax.broadcasted_iota(I32, (8, 128), 0)
    lane = lax.broadcasted_iota(I32, (8, 128), 1)
    low = row < 4
    half = jnp.where(low, 0, 1)
    left = lane < 64

    def spread(ref, r):
        return jnp.broadcast_to(ref[pl.ds(r, 1), :], (8, 128))

    def halves(ref, r, c):
        a = ref[pl.ds(r, 1), pl.ds(256 * c, 128)]
        b = ref[pl.ds(r, 1), pl.ds(256 * c + 128, 128)]
        return jnp.where(low, jnp.broadcast_to(a, (8, 128)), jnp.broadcast_to(b, (8, 128)))

    def entries(k):
        if k < 4:
            a = dom_ref[pl.ds(1 + k // 2, 1), pl.ds(128 * (k % 2), 128)]
            return jnp.broadcast_to(a, (8, 128))
        if k < 6:
            return jnp.broadcast_to(sub_ref[pl.ds(k - 4, 1), :], (8, 128))
        a = jnp.broadcast_to(dom_ref[pl.ds(0, 1), pl.ds(0, 128)], (8, 128))
        b = jnp.broadcast_to(dom_ref[pl.ds(3, 1), pl.ds(0, 128)], (8, 128))
        return jnp.where(left, a, pltpu.roll(b, 64, 1))

    def valid(k):
        if k < 4:
            return lane + 128 * (k % 2) < cnt_ref[1 + k // 2]
        if k < 6:
            return lane >= 0
        return jnp.where(left, lane, lane - 64) < jnp.where(left, cnt_ref[0], cnt_ref[3])

    for load in loads[:3]:
        load.wait()
    for k in range(7):
        e = entries(k)
        ehi[k] = lax.shift_right_logical(e, 7)
        elo[k] = lax.bitwise_and(e, 127)
    for c in range(2):
        for n in range(27):
            parts = [lam_ref[n, :, pl.ds(256 * c + 128 * h, 128)] for h in range(2)]
            xs[0, c, n] = jnp.concatenate(parts, axis=0)

    def prepare():
        for load in loads[3:]:
            load.wait()
        for c in range(2):
            mean = None
            for n in range(27):
                v = halves(visc_ref, n, c)
                vb[c, n] = v
                w = float(WEIGHTS[n // 9] * WEIGHTS[n // 3 % 3] * WEIGHTS[n % 3])
                mean = v * w if mean is None else mean + v * w
            mean = mean * 0.125
            inv = halves(inv_ref, 0, c)
            invb[c] = inv
            hmv[c] = 0.5 * mean
            for d in range(3):
                speed = halves(vel_ref, d, c)
                velb[c, d] = speed
                for s in range(2):
                    outward = speed if s == 0 else -speed
                    rate[2 * (2 * d + s) + c] = jnp.minimum(outward, 0.0) + 2.0 * (mean * inv)

        wide = lax.broadcasted_iota(I32, (128, 128), 0)
        found = jnp.zeros((48, 128), F32)
        for k in range(7):
            e = entries(k)
            hi = lax.shift_right_logical(e, 7)
            lo = lax.bitwise_and(e, 127)
            ok = valid(k)
            where_row = [jnp.where((hi == row + 8 * b) & ok, 1.0, 0.0) for b in range(3)]
            lane_f = lane.astype(F32)
            left_rows = [x * float(k + 1) for x in where_row] + [x * lane_f for x in where_row]
            a = jnp.concatenate(left_rows, axis=0).astype(jnp.bfloat16)
            b = jnp.where(jnp.concatenate([lo] * 16, axis=0) == wide, 1.0, 0.0).astype(jnp.bfloat16)
            found = found + lax.dot_general(
                a, b, (((1,), (1,)), ((), ())), preferred_element_type=F32
            )
        nat[...] = found.astype(I32)

        for f in range(6):
            for c in range(2):
                g = 2 * f + c
                ra, rb = 4 * f + 2 * c, 4 * f + 2 * c + 1
                p = jnp.where(low, spread(part_ref, ra), spread(part_ref, rb))
                r = lax.shift_right_logical(p, 7)
                swap = lax.bitwise_xor(lax.bitwise_and(r, 1), half)
                ihi[g] = swap * 12 + lax.shift_right_logical(r, 1)
                ilo[g] = lax.bitwise_and(p, 127)
                rhi[g] = jnp.where(low, spread(nat, ra), spread(nat, rb))
                rlo[g] = jnp.where(low, spread(nat, 24 + ra), spread(nat, 24 + rb))
                ori[g] = jnp.where(low, spread(orient_ref, ra), spread(orient_ref, rb))

    def put_table(f, c, values):
        g = 2 * f + c
        swapped = [pltpu.roll(x, 4, 0) for x in values]
        for q in range(9):
            tab[g, q] = values[q]
            tab[12 + g, q] = swapped[q]
        for k in range(5):
            if k < 4:
                tp[4 * f + 2 * c, k] = jnp.where(low, values[2 * k], swapped[2 * k + 1])
                tp[4 * f + 2 * c + 1, k] = jnp.where(low, swapped[2 * k], values[2 * k + 1])
            else:
                tp[4 * f + 2 * c, k] = values[8]
                tp[4 * f + 2 * c + 1, k] = swapped[8]

    def copies(rnd):
        plan = [
            (sfar.at[rnd, 0], rfar.at[rnd, 1], "dom", -2),
            (sfar.at[rnd, 1], rfar.at[rnd, 0], "dom", 2),
        ]
        for part in range(2):
            piece = pl.ds(5 * part, 5)
            plan.append((snear.at[rnd, 0, piece], rnear.at[rnd, 1, piece], "dom", -1))
            plan.append((snear.at[rnd, 1, piece], rnear.at[rnd, 0, piece], "dom", 1))
        plan.append((ssub.at[rnd, 0], rsub.at[rnd, 1], "sub", -1))
        plan.append((ssub.at[rnd, 1], rsub.at[rnd, 0], "sub", 1))
        made = []
        for i, (src, dst, axis, by) in enumerate(plan):
            copy = pltpu.make_async_remote_copy(
                src_ref=src,
                dst_ref=dst,
                send_sem=send_sem.at[rnd, i],
                recv_sem=recv_sem.at[rnd, i],
                device_id=at_dom(by) if axis == "dom" else at_sub(by),
                device_id_type=MESH,
            )
            made.append((copy, axis, by))
        return made

    def start(entry):
        copy, axis, by = entry
        if axis == "sub":
            copy.start()
        else:
            pl.when(has_dom(by))(copy.start)

    def wait_in(entry):
        copy, axis, by = entry
        if axis == "sub":
            copy.wait_recv()
        else:
            pl.when(has_dom(-by))(copy.wait_recv)

    def wait_out(entry):
        copy, axis, by = entry
        if axis == "sub":
            copy.wait_send()
        else:
            pl.when(has_dom(by))(copy.wait_send)

    def collect(k):
        hi, lo = ehi[k], elo[k]
        total = [None] * 5
        for s in range(24):
            here = hi == s
            for m in range(5):
                x = lanes(tp[s, m], lo)
                total[m] = x if s == 0 else jnp.where(here, x, total[m])
        return total

    def send(rnd):
        out = copies(rnd)
        x = collect(6)
        for m in range(3):
            a = x[2 * m]
            if m < 2:
                b = x[2 * m + 1]
                sfar[rnd, 0, m] = jnp.where(left, a, pltpu.roll(b, 64, 1))
                sfar[rnd, 1, m] = jnp.where(left, pltpu.roll(a, 64, 1), b)
            else:
                sfar[rnd, 0, m] = a
                sfar[rnd, 1, m] = pltpu.roll(a, 64, 1)

        @pl.when(rnd == 0)
        def _():
            pl.semaphore_wait(barrier, partners)

        start(out[0])
        start(out[1])
        for part in range(2):
            for side in range(2):
                x = collect(2 * side + part)
                for m in range(5):
                    snear[rnd, side, 5 * part + m] = x[m]
                start(out[2 + 2 * part + side])
        for side in range(2):
            x = collect(4 + side)
            for m in range(5):
                ssub[rnd, side, m] = x[m]
            start(out[6 + side])

    def gathered(g):
        hi, lo = ihi[g], ilo[g]
        total = [None] * 9
        for s in range(24):
            here = hi == s
            for q in range(9):
                x = lanes(tab[s, q], lo)
                total[q] = x if s == 0 else jnp.where(here, x, total[q])
        return total

    def local_first(into):
        depth = lax.broadcasted_iota(I32, (128, 128), 0).astype(jnp.int16)

        def groups(b, carry):
            for u in range(6):
                g = 6 * b + u
                total = gathered(g)
                for q in range(9):
                    into[g, q] = total[q]
            for u in range(2):
                j = 2 * b + u
                wanted = jnp.broadcast_to(part_ref[pl.ds(20 + j, 1), :], (128, 128))
                wanted = wanted.astype(jnp.int16)
                one = jnp.ones((128, 128), jnp.bfloat16)
                zero = jnp.zeros((128, 128), jnp.bfloat16)
                for i in range(24):
                    place = wanted == depth + jnp.int16(128 * i)
                    picks[b, pl.ds(128 * i, 128), pl.ds(128 * u, 128)] = jnp.where(
                        place, one, zero
                    )
            return carry

        lax.fori_loop(0, 2, groups, 0)

    def local_later(into):
        zero = jnp.zeros((8, 128), F32)
        for r in range(24):
            words = [tp[r, m] for m in range(5)] + [zero]
            for m in range(3):
                x = jnp.concatenate(words[2 * m : 2 * m + 2], axis=0)
                high = x.astype(jnp.bfloat16)
                rest = (x - high.astype(F32)).astype(jnp.bfloat16)
                split[pl.ds(16 * m, 16), pl.ds(128 * r, 128)] = high
                split[pl.ds(48 + 16 * m, 16), pl.ds(128 * r, 128)] = rest
        for c in range(2):
            for u in range(5):
                g = 5 * c + u
                total = gathered(g)
                for q in range(9):
                    into[g, q] = total[q]
            both = jnp.dot(split[...], picks[c], preferred_element_type=F32)
            value = both[:48] + both[48:]
            g = 10 + c
            for m in range(5):
                x, y = [value[8 * m : 8 * m + 8, 128 * h : 128 * h + 128] for h in range(2)]
                into[g, 2 * m] = jnp.where(low, x, pltpu.roll(y, 4, 0))
                if m < 4:
                    into[g, 2 * m + 1] = jnp.where(low, pltpu.roll(x, 4, 0), y)

    def double(k, words):
        for m in range(5):
            x = words[m]
            y = pltpu.roll(x, 4, 0)
            dup[k, 2 * m] = jnp.where(low, x, y)
            if m < 4:
                dup[k, 2 * m + 1] = jnp.where(low, y, x)

    def merged(total, g, lists):
        hi, lo = rhi[g], rlo[g]
        for k in lists:
            here = hi == k + 1
            for q in range(9):
                total[q] = jnp.where(here, lanes(dup[k, q], lo), total[q])
        return total

    def arrive(rnd, into, difference):
        moved = copies(rnd)
        for entry in moved[6:]:
            wait_in(entry)
        for k in range(2):
            double(4 + k, [rsub[rnd, k, m] for m in range(5)])

        def merge(lists):
            for g in range(12):
                total = merged([into[g, q] for q in range(9)], g, lists)
                for q in range(9):
                    into[g, q] = total[q]

        merge([4, 5])
        for entry in moved[2:4]:
            wait_in(entry)
        for k in (0, 2):
            double(k, [rnear[rnd, k // 2, m] for m in range(5)])
        merge([0, 2])
        for entry in moved[4:6] + moved[:2]:
            wait_in(entry)
        for k in (1, 3):
            double(k, [rnear[rnd, k // 2, 5 + m] for m in range(5)])
        far = []
        for m in range(3):
            a, b = rfar[rnd, 0, m], rfar[rnd, 1, m]
            far.append(jnp.where(left, a, pltpu.roll(b, 64, 1)))
            if m < 2:
                far.append(jnp.where(left, pltpu.roll(a, 64, 1), b))
        double(6, far)

        def last(b, carry):
            for u in range(6):
                g = 6 * b + u
                code = ori[g]
                total = merged([into[g, q] for q in range(9)], g, [1, 3, 6])
                flip_i = lax.bitwise_and(code, 1) == 1
                flip_j = lax.bitwise_and(code, 2) == 2
                swap = lax.bitwise_and(code, 4) == 4
                for j in range(3):
                    x, y = total[j], total[6 + j]
                    total[j] = jnp.where(flip_i, y, x)
                    total[6 + j] = jnp.where(flip_i, x, y)
                for i in range(3):
                    x, y = total[3 * i], total[3 * i + 2]
                    total[3 * i] = jnp.where(flip_j, y, x)
                    total[3 * i + 2] = jnp.where(flip_j, x, y)
                for i in range(3):
                    for j in range(i):
                        x, y = total[3 * i + j], total[3 * j + i]
                        total[3 * i + j] = jnp.where(swap, y, x)
                        total[3 * j + i] = jnp.where(swap, x, y)
                for q in range(9):
                    own = tab[g, q]
                    into[g, q] = total[q] - own if difference else total[q] + own
            return carry

        lax.fori_loop(0, 2, last, 0)

    def segment(seg, carry):
        def traces(c, carry):
            for d in range(3):
                face = ([], [])
                for q in range(9):
                    x = [xs[seg, c, node(d, k, q)] for k in range(3)]
                    for s in range(2):
                        face[s].append(combine(ENDS[s], x))
                for s in range(2):
                    put_table(2 * d + s, c, face[s])
            return carry

        lax.fori_loop(0, 2, traces, 0)
        send(2 * seg)
        pl.when(seg == 0)(prepare)
        pl.when(seg == 0)(functools.partial(local_first, jmp))
        pl.when(seg != 0)(functools.partial(local_later, jmp))
        arrive(2 * seg, jmp, True)

        def gradients(c, carry):
            inv = invb[c]
            for d in range(3):
                face = ([], [])
                for q in range(9):
                    x = [xs[seg, c, node(d, k, q)] for k in range(3)]
                    jumps = [jmp[2 * (2 * d + s) + c, q] for s in range(2)]
                    g = []
                    for k in range(3):
                        lift = [0.5 * SIGNS[s] * ENDS[s][k] / WEIGHTS[k] for s in range(2)]
                        g.append(inv * combine(list(DERIV[k]) + lift, x + jumps))
                        grd[c, d, 3 * q + k] = g[k]
                    for s in range(2):
                        face[s].append(combine(SIGNS[s] * ENDS[s], g))
                for s in range(2):
                    put_table(2 * d + s, c, face[s])
            return carry

        lax.fori_loop(0, 2, gradients, 0)
        send(2 * seg + 1)
        local_later(nsum)
        arrive(2 * seg + 1, nsum, False)

        def advance(c):
            inv, drag = invb[c], hmv[c]
            total = [None] * 27
            for d in range(3):
                speed = velb[c, d]
                rates = [rate[2 * (2 * d + s) + c] for s in range(2)]
                for q in range(9):
                    flux = []
                    for k in range(3):
                        n = node(d, k, q)
                        flux.append(vb[c, n] * grd[c, d, 3 * q + k] - speed * xs[seg, c, n])
                    surface = []
                    for s in range(2):
                        g = 2 * (2 * d + s) + c
                        surface.append(rates[s] * jmp[g, q] - drag * nsum[g, q])
                    for k in range(3):
                        n = node(d, k, q)
                        lift = [ENDS[s][k] / WEIGHTS[k] for s in range(2)]
                        term = combine(list(DERIV[k]) + lift, flux + surface)
                        total[n] = term if total[n] is None else total[n] + term
            scale = STEP * inv
            for n in range(27):
                new = xs[seg, c, n] + scale * total[n]
                xs[seg + 1, c, n] = new
                result = 0.5 * (xs[0, c, n] + new)
                for h in range(2):
                    out_ref[n, :, pl.ds(256 * c + 128 * h, 128)] = result[4 * h : 4 * h + 4]

        advance(0)
        advance(1)
        return carry

    lax.fori_loop(0, 2, segment, 0)

    def drain(rnd, carry):
        for entry in copies(rnd):
            wait_out(entry)
        return carry

    lax.fori_loop(0, 4, drain, 0)


def on_device(
    n_dom,
    n_sub,
    adjoint_in,
    viscosity,
    velocity,
    inverse_size,
    local_partner,
    face_orient,
    dom_counts,
    dom_slots,
    sub_slots,
):
    lam = adjoint_in.transpose(1, 0, 2)
    vmem = pl.BlockSpec(memory_space=pltpu.VMEM)
    tile = (8, 128)
    out = pl.pallas_call(
        functools.partial(kernel, n_dom, n_sub),
        out_shape=jax.ShapeDtypeStruct((27, 4, 512), F32),
        in_specs=[pl.BlockSpec(memory_space=pl.ANY)] * 9,
        out_specs=vmem,
        scratch_shapes=[
            pltpu.VMEM((27, 4, 512), F32),
            pltpu.VMEM((27, 512), F32),
            pltpu.VMEM((3, 512), F32),
            pltpu.VMEM((1, 512), F32),
            pltpu.VMEM((24, 128), I32),
            pltpu.VMEM((24, 128), I32),
            pltpu.SMEM((4,), I32),
            pltpu.VMEM((4, 256), I32),
            pltpu.VMEM((2, 128), I32),
            pltpu.SemaphoreType.DMA((9,)),
            pltpu.VMEM((3, 2, 27) + tile, F32),
            pltpu.VMEM((2, 27) + tile, F32),
            pltpu.VMEM((2, 3) + tile, F32),
            pltpu.VMEM((2,) + tile, F32),
            pltpu.VMEM((2,) + tile, F32),
            pltpu.VMEM((12,) + tile, F32),
            pltpu.VMEM((24, 9) + tile, F32),
            pltpu.VMEM((24, 5) + tile, F32),
            pltpu.VMEM((12, 9) + tile, F32),
            pltpu.VMEM((12, 9) + tile, F32),
            pltpu.VMEM((2, 3, 27) + tile, F32),
            pltpu.VMEM((7,) + tile, I32),
            pltpu.VMEM((7,) + tile, I32),
            pltpu.VMEM((12,) + tile, I32),
            pltpu.VMEM((12,) + tile, I32),
            pltpu.VMEM((12,) + tile, I32),
            pltpu.VMEM((12,) + tile, I32),
            pltpu.VMEM((12,) + tile, I32),
            pltpu.VMEM((48, 128), I32),
            pltpu.VMEM((7, 9) + tile, F32),
            pltpu.VMEM((2, 3072, 256), jnp.bfloat16),
            pltpu.VMEM((96, 3072), jnp.bfloat16),
            pltpu.VMEM((4, 2, 10) + tile, F32),
            pltpu.VMEM((4, 2, 5) + tile, F32),
            pltpu.VMEM((4, 2, 3) + tile, F32),
            pltpu.VMEM((4, 2, 10) + tile, F32),
            pltpu.VMEM((4, 2, 5) + tile, F32),
            pltpu.VMEM((4, 2, 3) + tile, F32),
            pltpu.SemaphoreType.DMA((4, 8)),
            pltpu.SemaphoreType.DMA((4, 8)),
        ],
        compiler_params=pltpu.CompilerParams(collective_id=0, has_side_effects=True, vmem_limit_bytes=24 << 20),
        name="segments",
    )(
        *(
            pltpu.with_memory_space_constraint(x, pltpu.HBM)
            for x in (
                lam,
                viscosity,
                velocity,
                inverse_size.reshape(1, 512),
                local_partner.reshape(24, 128),
                face_orient.reshape(24, 128),
                dom_counts.reshape(4),
                dom_slots.reshape(4, 256),
                sub_slots.reshape(2, 128),
            )
        )
    )
    return out.transpose(1, 0, 2)


def solution(mesh):
    in_specs = (
        P(None, None, ("dom", "sub")),
        P(None, ("dom", "sub")),
        P(None, ("dom", "sub")),
        P(("dom", "sub")),
        P("dom", "sub", None),
        P("dom", "sub", None),
        P("dom", "sub", None),
        P("dom", "sub", None, None),
        P("dom", "sub", None, None),
    )
    return jax.shard_map(
        functools.partial(on_device, mesh.shape["dom"], mesh.shape["sub"]),
        mesh=mesh,
        in_specs=in_specs,
        out_specs=P(None, None, ("dom", "sub")),
        check_vma=False,
    )
```

```python
import functools

import jax
import jax.numpy as jnp
import numpy as np
from jax import lax
from jax.experimental import pallas as pl
from jax.experimental.pallas import tpu as pltpu
from jax.sharding import PartitionSpec as P

MESH = pl.DeviceIdType.MESH
STEP = 0.02
F32 = jnp.float32
I32 = jnp.int32


def line_tables():
    points = np.array([-np.sqrt(0.6), 0.0, np.sqrt(0.6)])
    weights = np.array([5.0, 8.0, 5.0]) / 9.0

    def lagrange(at):
        values = np.ones(3)
        for j in range(3):
            for m in range(3):
                if m != j:
                    values[j] *= (at - points[m]) / (points[j] - points[m])
        return values

    derivative = np.zeros((3, 3))
    for i in range(3):
        for j in range(3):
            for k in range(3):
                if k != j:
                    term = 1.0 / (points[j] - points[k])
                    for m in range(3):
                        if m != j and m != k:
                            term *= (points[i] - points[m]) / (points[j] - points[m])
                    derivative[i, j] += term
    derivative[1, 1] = 0.0
    return derivative, (lagrange(-1.0), lagrange(1.0)), weights


DERIV, ENDS, WEIGHTS = line_tables()
SIGNS = (-1.0, 1.0)


def node(d, k, q):
    i, j = divmod(q, 3)
    at = [i, j]
    at.insert(d, k)
    return 9 * at[0] + 3 * at[1] + at[2]


def combine(coefficients, values):
    total = None
    for a, x in zip(coefficients, values):
        a = float(a)
        if a == 0.0:
            continue
        term = x if a == 1.0 else x * a
        total = term if total is None else total + term
    return total


def lanes(x, index):
    return jnp.take_along_axis(x, index, axis=1)


def kernel(
    n_dom,
    n_sub,
    lam_in,
    visc_in,
    vel_in,
    inv_in,
    part_in,
    orient_in,
    cnt_in,
    dom_in,
    sub_in,
    out_ref,
    lam_ref,
    visc_ref,
    vel_ref,
    inv_ref,
    part_ref,
    orient_ref,
    cnt_ref,
    dom_ref,
    sub_ref,
    in_sem,
    xs,
    vb,
    velb,
    invb,
    hmv,
    rate,
    tab,
    tp,
    jmp,
    nsum,
    grd,
    ehi,
    elo,
    ihi,
    ilo,
    rhi,
    rlo,
    ori,
    nat,
    dup,
    picks,
    split,
    snear,
    ssub,
    sfar,
    rnear,
    rsub,
    rfar,
    send_sem,
    recv_sem,
):
    dom = lax.axis_index("dom")
    sub = lax.axis_index("sub")

    def at_dom(by):
        return (lax.rem(dom + by + n_dom, n_dom), sub)

    def has_dom(by):
        return dom + by >= 0 if by < 0 else dom + by < n_dom

    def at_sub(by):
        return (dom, lax.rem(sub + by + n_sub, n_sub))

    arrays = (
        (lam_in, lam_ref),
        (dom_in, dom_ref),
        (sub_in, sub_ref),
        (cnt_in, cnt_ref),
        (part_in, part_ref),
        (orient_in, orient_ref),
        (visc_in, visc_ref),
        (vel_in, vel_ref),
        (inv_in, inv_ref),
    )
    loads = [
        pltpu.make_async_copy(src, dst, in_sem.at[i]) for i, (src, dst) in enumerate(arrays)
    ]
    for load in loads:
        load.start()

    barrier = pltpu.get_barrier_semaphore()
    partners = 2
    for by in (-2, 2, -1, 1):
        partners = partners + jnp.where(has_dom(by), 1, 0)

        @pl.when(has_dom(by))
        def _(by=by):
            pl.semaphore_signal(barrier, inc=1, device_id=at_dom(by), device_id_type=MESH)

    for by in (-1, 1):
        pl.semaphore_signal(barrier, inc=1, device_id=at_sub(by), device_id_type=MESH)

    row = lax.broadcasted_iota(I32, (8, 128), 0)
    lane = lax.broadcasted_iota(I32, (8, 128), 1)
    low = row < 4
    half = jnp.where(low, 0, 1)
    left = lane < 64

    def spread(ref, r):
        return jnp.broadcast_to(ref[pl.ds(r, 1), :], (8, 128))

    def halves(ref, r, c):
        a = ref[pl.ds(r, 1), pl.ds(256 * c, 128)]
        b = ref[pl.ds(r, 1), pl.ds(256 * c + 128, 128)]
        return jnp.where(low, jnp.broadcast_to(a, (8, 128)), jnp.broadcast_to(b, (8, 128)))

    def entries(k):
        if k < 4:
            a = dom_ref[pl.ds(1 + k // 2, 1), pl.ds(128 * (k % 2), 128)]
            return jnp.broadcast_to(a, (8, 128))
        if k < 6:
            return jnp.broadcast_to(sub_ref[pl.ds(k - 4, 1), :], (8, 128))
        a = jnp.broadcast_to(dom_ref[pl.ds(0, 1), pl.ds(0, 128)], (8, 128))
        b = jnp.broadcast_to(dom_ref[pl.ds(3, 1), pl.ds(0, 128)], (8, 128))
        return jnp.where(left, a, pltpu.roll(b, 64, 1))

    def valid(k):
        if k < 4:
            return lane + 128 * (k % 2) < cnt_ref[1 + k // 2]
        if k < 6:
            return lane >= 0
        return jnp.where(left, lane, lane - 64) < jnp.where(left, cnt_ref[0], cnt_ref[3])

    for load in loads[:3]:
        load.wait()
    for k in range(7):
        e = entries(k)
        ehi[k] = lax.shift_right_logical(e, 7)
        elo[k] = lax.bitwise_and(e, 127)
    for c in range(2):
        for n in range(27):
            parts = [lam_ref[n, :, pl.ds(256 * c + 128 * h, 128)] for h in range(2)]
            xs[0, c, n] = jnp.concatenate(parts, axis=0)

    def prepare():
        for load in loads[3:]:
            load.wait()
        for c in range(2):
            mean = None
            for n in range(27):
                v = halves(visc_ref, n, c)
                vb[c, n] = v
                w = float(WEIGHTS[n // 9] * WEIGHTS[n // 3 % 3] * WEIGHTS[n % 3])
                mean = v * w if mean is None else mean + v * w
            mean = mean * 0.125
            inv = halves(inv_ref, 0, c)
            invb[c] = inv
            hmv[c] = 0.5 * mean
            for d in range(3):
                speed = halves(vel_ref, d, c)
                velb[c, d] = speed
                for s in range(2):
                    outward = speed if s == 0 else -speed
                    rate[2 * (2 * d + s) + c] = jnp.minimum(outward, 0.0) + 2.0 * (mean * inv)

        wide = lax.broadcasted_iota(I32, (128, 128), 0)
        found = jnp.zeros((48, 128), F32)
        for k in range(7):
            e = entries(k)
            hi = lax.shift_right_logical(e, 7)
            lo = lax.bitwise_and(e, 127)
            ok = valid(k)
            where_row = [jnp.where((hi == row + 8 * b) & ok, 1.0, 0.0) for b in range(3)]
            lane_f = lane.astype(F32)
            left_rows = [x * float(k + 1) for x in where_row] + [x * lane_f for x in where_row]
            a = jnp.concatenate(left_rows, axis=0).astype(jnp.bfloat16)
            b = jnp.where(jnp.concatenate([lo] * 16, axis=0) == wide, 1.0, 0.0).astype(jnp.bfloat16)
            found = found + lax.dot_general(
                a, b, (((1,), (1,)), ((), ())), preferred_element_type=F32
            )
        nat[...] = found.astype(I32)

        for f in range(6):
            for c in range(2):
                g = 2 * f + c
                ra, rb = 4 * f + 2 * c, 4 * f + 2 * c + 1
                p = jnp.where(low, spread(part_ref, ra), spread(part_ref, rb))
                r = lax.shift_right_logical(p, 7)
                swap = lax.bitwise_xor(lax.bitwise_and(r, 1), half)
                ihi[g] = swap * 12 + lax.shift_right_logical(r, 1)
                ilo[g] = lax.bitwise_and(p, 127)
                rhi[g] = jnp.where(low, spread(nat, ra), spread(nat, rb))
                rlo[g] = jnp.where(low, spread(nat, 24 + ra), spread(nat, 24 + rb))
                ori[g] = jnp.where(low, spread(orient_ref, ra), spread(orient_ref, rb))

    def put_table(f, c, values):
        g = 2 * f + c
        swapped = [pltpu.roll(x, 4, 0) for x in values]
        for q in range(9):
            tab[g, q] = values[q]
            tab[12 + g, q] = swapped[q]
        for k in range(5):
            if k < 4:
                tp[4 * f + 2 * c, k] = jnp.where(low, values[2 * k], swapped[2 * k + 1])
                tp[4 * f + 2 * c + 1, k] = jnp.where(low, swapped[2 * k], values[2 * k + 1])
            else:
                tp[4 * f + 2 * c, k] = values[8]
                tp[4 * f + 2 * c + 1, k] = swapped[8]

    def copies(rnd):
        plan = [
            (sfar.at[rnd, 0], rfar.at[rnd, 1], "dom", -2),
            (sfar.at[rnd, 1], rfar.at[rnd, 0], "dom", 2),
        ]
        for part in range(2):
            piece = pl.ds(5 * part, 5)
            plan.append((snear.at[rnd, 0, piece], rnear.at[rnd, 1, piece], "dom", -1))
            plan.append((snear.at[rnd, 1, piece], rnear.at[rnd, 0, piece], "dom", 1))
        plan.append((ssub.at[rnd, 0], rsub.at[rnd, 1], "sub", -1))
        plan.append((ssub.at[rnd, 1], rsub.at[rnd, 0], "sub", 1))
        made = []
        for i, (src, dst, axis, by) in enumerate(plan):
            copy = pltpu.make_async_remote_copy(
                src_ref=src,
                dst_ref=dst,
                send_sem=send_sem.at[rnd, i],
                recv_sem=recv_sem.at[rnd, i],
                device_id=at_dom(by) if axis == "dom" else at_sub(by),
                device_id_type=MESH,
            )
            made.append((copy, axis, by))
        return made

    def start(entry):
        copy, axis, by = entry
        if axis == "sub":
            copy.start()
        else:
            pl.when(has_dom(by))(copy.start)

    def wait_in(entry):
        copy, axis, by = entry
        if axis == "sub":
            copy.wait_recv()
        else:
            pl.when(has_dom(-by))(copy.wait_recv)

    def wait_out(entry):
        copy, axis, by = entry
        if axis == "sub":
            copy.wait_send()
        else:
            pl.when(has_dom(by))(copy.wait_send)

    def collect(k):
        hi, lo = ehi[k], elo[k]
        total = [None] * 5
        for s in range(24):
            here = hi == s
            for m in range(5):
                x = lanes(tp[s, m], lo)
                total[m] = x if s == 0 else jnp.where(here, x, total[m])
        return total

    def send(rnd):
        out = copies(rnd)
        x = collect(6)
        for m in range(3):
            a = x[2 * m]
            if m < 2:
                b = x[2 * m + 1]
                sfar[rnd, 0, m] = jnp.where(left, a, pltpu.roll(b, 64, 1))
                sfar[rnd, 1, m] = jnp.where(left, pltpu.roll(a, 64, 1), b)
            else:
                sfar[rnd, 0, m] = a
                sfar[rnd, 1, m] = pltpu.roll(a, 64, 1)

        @pl.when(rnd == 0)
        def _():
            pl.semaphore_wait(barrier, partners)

        start(out[0])
        start(out[1])
        for part in range(2):
            for side in range(2):
                x = collect(2 * side + part)
                for m in range(5):
                    snear[rnd, side, 5 * part + m] = x[m]
        for entry in out[2:6]:
            start(entry)
        for side in range(2):
            x = collect(4 + side)
            for m in range(5):
                ssub[rnd, side, m] = x[m]
        for entry in out[6:]:
            start(entry)

    def gathered(g):
        hi, lo = ihi[g], ilo[g]
        total = [None] * 9
        for s in range(24):
            here = hi == s
            for q in range(9):
                x = lanes(tab[s, q], lo)
                total[q] = x if s == 0 else jnp.where(here, x, total[q])
        return total

    def local_first(into):
        depth = lax.broadcasted_iota(I32, (128, 128), 0).astype(jnp.int16)

        def groups(b, carry):
            for u in range(6):
                g = 6 * b + u
                total = gathered(g)
                for q in range(9):
                    into[g, q] = total[q]
            for u in range(2):
                j = 2 * b + u
                wanted = jnp.broadcast_to(part_ref[pl.ds(20 + j, 1), :], (128, 128))
                wanted = wanted.astype(jnp.int16)
                one = jnp.ones((128, 128), jnp.bfloat16)
                zero = jnp.zeros((128, 128), jnp.bfloat16)
                for i in range(24):
                    place = wanted == depth + jnp.int16(128 * i)
                    picks[b, pl.ds(128 * i, 128), pl.ds(128 * u, 128)] = jnp.where(
                        place, one, zero
                    )
            return carry

        lax.fori_loop(0, 2, groups, 0)

    def local_later(into):
        zero = jnp.zeros((8, 128), F32)
        for r in range(24):
            words = [tp[r, m] for m in range(5)] + [zero]
            for m in range(3):
                x = jnp.concatenate(words[2 * m : 2 * m + 2], axis=0)
                high = x.astype(jnp.bfloat16)
                rest = (x - high.astype(F32)).astype(jnp.bfloat16)
                split[pl.ds(16 * m, 16), pl.ds(128 * r, 128)] = high
                split[pl.ds(48 + 16 * m, 16), pl.ds(128 * r, 128)] = rest
        for c in range(2):
            for u in range(5):
                g = 5 * c + u
                total = gathered(g)
                for q in range(9):
                    into[g, q] = total[q]
            both = jnp.dot(split[...], picks[c], preferred_element_type=F32)
            value = both[:48] + both[48:]
            g = 10 + c
            for m in range(5):
                x, y = [value[8 * m : 8 * m + 8, 128 * h : 128 * h + 128] for h in range(2)]
                into[g, 2 * m] = jnp.where(low, x, pltpu.roll(y, 4, 0))
                if m < 4:
                    into[g, 2 * m + 1] = jnp.where(low, pltpu.roll(x, 4, 0), y)

    def double(k, words):
        for m in range(5):
            x = words[m]
            y = pltpu.roll(x, 4, 0)
            dup[k, 2 * m] = jnp.where(low, x, y)
            if m < 4:
                dup[k, 2 * m + 1] = jnp.where(low, y, x)

    def merged(total, g, lists):
        hi, lo = rhi[g], rlo[g]
        for k in lists:
            here = hi == k + 1
            for q in range(9):
                total[q] = jnp.where(here, lanes(dup[k, q], lo), total[q])
        return total

    def arrive(rnd, into, difference):
        moved = copies(rnd)
        for entry in moved[6:]:
            wait_in(entry)
        for k in range(2):
            double(4 + k, [rsub[rnd, k, m] for m in range(5)])

        def merge(lists):
            for g in range(12):
                total = merged([into[g, q] for q in range(9)], g, lists)
                for q in range(9):
                    into[g, q] = total[q]

        for entry in moved[:2]:
            wait_in(entry)
        far = []
        for m in range(3):
            a, b = rfar[rnd, 0, m], rfar[rnd, 1, m]
            far.append(jnp.where(left, a, pltpu.roll(b, 64, 1)))
            if m < 2:
                far.append(jnp.where(left, pltpu.roll(a, 64, 1), b))
        double(6, far)
        merge([4, 5, 6])
        for entry in moved[2:6]:
            wait_in(entry)
        for k in range(4):
            double(k, [rnear[rnd, k // 2, 5 * (k % 2) + m] for m in range(5)])

        def last(b, carry):
            for u in range(6):
                g = 6 * b + u
                code = ori[g]
                total = merged([into[g, q] for q in range(9)], g, range(4))
                flip_i = lax.bitwise_and(code, 1) == 1
                flip_j = lax.bitwise_and(code, 2) == 2
                swap = lax.bitwise_and(code, 4) == 4
                for j in range(3):
                    x, y = total[j], total[6 + j]
                    total[j] = jnp.where(flip_i, y, x)
                    total[6 + j] = jnp.where(flip_i, x, y)
                for i in range(3):
                    x, y = total[3 * i], total[3 * i + 2]
                    total[3 * i] = jnp.where(flip_j, y, x)
                    total[3 * i + 2] = jnp.where(flip_j, x, y)
                for i in range(3):
                    for j in range(i):
                        x, y = total[3 * i + j], total[3 * j + i]
                        total[3 * i + j] = jnp.where(swap, y, x)
                        total[3 * j + i] = jnp.where(swap, x, y)
                for q in range(9):
                    own = tab[g, q]
                    into[g, q] = total[q] - own if difference else total[q] + own
            return carry

        lax.fori_loop(0, 2, last, 0)

    def segment(seg, carry):
        def traces(c, carry):
            for d in range(3):
                face = ([], [])
                for q in range(9):
                    x = [xs[seg, c, node(d, k, q)] for k in range(3)]
                    for s in range(2):
                        face[s].append(combine(ENDS[s], x))
                for s in range(2):
                    put_table(2 * d + s, c, face[s])
            return carry

        lax.fori_loop(0, 2, traces, 0)
        send(2 * seg)
        pl.when(seg == 0)(prepare)
        pl.when(seg == 0)(functools.partial(local_first, jmp))
        pl.when(seg != 0)(functools.partial(local_later, jmp))
        arrive(2 * seg, jmp, True)

        def gradients(c, carry):
            inv = invb[c]
            for d in range(3):
                face = ([], [])
                for q in range(9):
                    x = [xs[seg, c, node(d, k, q)] for k in range(3)]
                    jumps = [jmp[2 * (2 * d + s) + c, q] for s in range(2)]
                    g = []
                    for k in range(3):
                        lift = [0.5 * SIGNS[s] * ENDS[s][k] / WEIGHTS[k] for s in range(2)]
                        g.append(inv * combine(list(DERIV[k]) + lift, x + jumps))
                        grd[c, d, 3 * q + k] = g[k]
                    for s in range(2):
                        face[s].append(combine(SIGNS[s] * ENDS[s], g))
                for s in range(2):
                    put_table(2 * d + s, c, face[s])
            return carry

        lax.fori_loop(0, 2, gradients, 0)
        send(2 * seg + 1)
        local_later(nsum)
        arrive(2 * seg + 1, nsum, False)

        def advance(c):
            inv, drag = invb[c], hmv[c]
            total = [None] * 27
            for d in range(3):
                speed = velb[c, d]
                rates = [rate[2 * (2 * d + s) + c] for s in range(2)]
                for q in range(9):
                    flux = []
                    for k in range(3):
                        n = node(d, k, q)
                        flux.append(vb[c, n] * grd[c, d, 3 * q + k] - speed * xs[seg, c, n])
                    surface = []
                    for s in range(2):
                        g = 2 * (2 * d + s) + c
                        surface.append(rates[s] * jmp[g, q] - drag * nsum[g, q])
                    for k in range(3):
                        n = node(d, k, q)
                        lift = [ENDS[s][k] / WEIGHTS[k] for s in range(2)]
                        term = combine(list(DERIV[k]) + lift, flux + surface)
                        total[n] = term if total[n] is None else total[n] + term
            scale = STEP * inv
            for n in range(27):
                new = xs[seg, c, n] + scale * total[n]
                xs[seg + 1, c, n] = new
                result = 0.5 * (xs[0, c, n] + new)
                for h in range(2):
                    out_ref[n, :, pl.ds(256 * c + 128 * h, 128)] = result[4 * h : 4 * h + 4]

        advance(0)
        advance(1)
        return carry

    lax.fori_loop(0, 2, segment, 0)

    def drain(rnd, carry):
        for entry in copies(rnd):
            wait_out(entry)
        return carry

    lax.fori_loop(0, 4, drain, 0)


def on_device(
    n_dom,
    n_sub,
    adjoint_in,
    viscosity,
    velocity,
    inverse_size,
    local_partner,
    face_orient,
    dom_counts,
    dom_slots,
    sub_slots,
):
    lam = adjoint_in.transpose(1, 0, 2)
    vmem = pl.BlockSpec(memory_space=pltpu.VMEM)
    tile = (8, 128)
    out = pl.pallas_call(
        functools.partial(kernel, n_dom, n_sub),
        out_shape=jax.ShapeDtypeStruct((27, 4, 512), F32),
        in_specs=[pl.BlockSpec(memory_space=pl.ANY)] * 9,
        out_specs=vmem,
        scratch_shapes=[
            pltpu.VMEM((27, 4, 512), F32),
            pltpu.VMEM((27, 512), F32),
            pltpu.VMEM((3, 512), F32),
            pltpu.VMEM((1, 512), F32),
            pltpu.VMEM((24, 128), I32),
            pltpu.VMEM((24, 128), I32),
            pltpu.SMEM((4,), I32),
            pltpu.VMEM((4, 256), I32),
            pltpu.VMEM((2, 128), I32),
            pltpu.SemaphoreType.DMA((9,)),
            pltpu.VMEM((3, 2, 27) + tile, F32),
            pltpu.VMEM((2, 27) + tile, F32),
            pltpu.VMEM((2, 3) + tile, F32),
            pltpu.VMEM((2,) + tile, F32),
            pltpu.VMEM((2,) + tile, F32),
            pltpu.VMEM((12,) + tile, F32),
            pltpu.VMEM((24, 9) + tile, F32),
            pltpu.VMEM((24, 5) + tile, F32),
            pltpu.VMEM((12, 9) + tile, F32),
            pltpu.VMEM((12, 9) + tile, F32),
            pltpu.VMEM((2, 3, 27) + tile, F32),
            pltpu.VMEM((7,) + tile, I32),
            pltpu.VMEM((7,) + tile, I32),
            pltpu.VMEM((12,) + tile, I32),
            pltpu.VMEM((12,) + tile, I32),
            pltpu.VMEM((12,) + tile, I32),
            pltpu.VMEM((12,) + tile, I32),
            pltpu.VMEM((12,) + tile, I32),
            pltpu.VMEM((48, 128), I32),
            pltpu.VMEM((7, 9) + tile, F32),
            pltpu.VMEM((2, 3072, 256), jnp.bfloat16),
            pltpu.VMEM((96, 3072), jnp.bfloat16),
            pltpu.VMEM((4, 2, 10) + tile, F32),
            pltpu.VMEM((4, 2, 5) + tile, F32),
            pltpu.VMEM((4, 2, 3) + tile, F32),
            pltpu.VMEM((4, 2, 10) + tile, F32),
            pltpu.VMEM((4, 2, 5) + tile, F32),
            pltpu.VMEM((4, 2, 3) + tile, F32),
            pltpu.SemaphoreType.DMA((4, 8)),
            pltpu.SemaphoreType.DMA((4, 8)),
        ],
        compiler_params=pltpu.CompilerParams(collective_id=0, has_side_effects=True, vmem_limit_bytes=24 << 20),
        name="segments",
    )(
        *(
            pltpu.with_memory_space_constraint(x, pltpu.HBM)
            for x in (
                lam,
                viscosity,
                velocity,
                inverse_size.reshape(1, 512),
                local_partner.reshape(24, 128),
                face_orient.reshape(24, 128),
                dom_counts.reshape(4),
                dom_slots.reshape(4, 256),
                sub_slots.reshape(2, 128),
            )
        )
    )
    return out.transpose(1, 0, 2)


def solution(mesh):
    in_specs = (
        P(None, None, ("dom", "sub")),
        P(None, ("dom", "sub")),
        P(None, ("dom", "sub")),
        P(("dom", "sub")),
        P("dom", "sub", None),
        P("dom", "sub", None),
        P("dom", "sub", None),
        P("dom", "sub", None, None),
        P("dom", "sub", None, None),
    )
    return jax.shard_map(
        functools.partial(on_device, mesh.shape["dom"], mesh.shape["sub"]),
        mesh=mesh,
        in_specs=in_specs,
        out_specs=P(None, None, ("dom", "sub")),
        check_vma=False,
    )
```

```python
import functools

import jax
import jax.numpy as jnp
import numpy as np
from jax import lax
from jax.experimental import pallas as pl
from jax.experimental.pallas import tpu as pltpu
from jax.sharding import PartitionSpec as P

MESH = pl.DeviceIdType.MESH
STEP = 0.02
F32 = jnp.float32
I32 = jnp.int32


def line_tables():
    points = np.array([-np.sqrt(0.6), 0.0, np.sqrt(0.6)])
    weights = np.array([5.0, 8.0, 5.0]) / 9.0

    def lagrange(at):
        values = np.ones(3)
        for j in range(3):
            for m in range(3):
                if m != j:
                    values[j] *= (at - points[m]) / (points[j] - points[m])
        return values

    derivative = np.zeros((3, 3))
    for i in range(3):
        for j in range(3):
            for k in range(3):
                if k != j:
                    term = 1.0 / (points[j] - points[k])
                    for m in range(3):
                        if m != j and m != k:
                            term *= (points[i] - points[m]) / (points[j] - points[m])
                    derivative[i, j] += term
    derivative[1, 1] = 0.0
    return derivative, (lagrange(-1.0), lagrange(1.0)), weights


DERIV, ENDS, WEIGHTS = line_tables()
SIGNS = (-1.0, 1.0)


def node(d, k, q):
    i, j = divmod(q, 3)
    at = [i, j]
    at.insert(d, k)
    return 9 * at[0] + 3 * at[1] + at[2]


def combine(coefficients, values):
    total = None
    for a, x in zip(coefficients, values):
        a = float(a)
        if a == 0.0:
            continue
        term = x if a == 1.0 else x * a
        total = term if total is None else total + term
    return total


def lanes(x, index):
    return jnp.take_along_axis(x, index, axis=1)


def kernel(
    n_dom,
    n_sub,
    lam_in,
    visc_in,
    vel_in,
    inv_in,
    part_in,
    orient_in,
    cnt_in,
    dom_in,
    sub_in,
    out_ref,
    lam_ref,
    visc_ref,
    vel_ref,
    inv_ref,
    part_ref,
    orient_ref,
    cnt_ref,
    dom_ref,
    sub_ref,
    in_sem,
    xs,
    vb,
    velb,
    invb,
    hmv,
    rate,
    tab,
    tp,
    jmp,
    nsum,
    grd,
    ehi,
    elo,
    ihi,
    ilo,
    rhi,
    rlo,
    ori,
    nat,
    dup,
    snear,
    ssub,
    sfar,
    rnear,
    rsub,
    rfar,
    send_sem,
    recv_sem,
):
    dom = lax.axis_index("dom")
    sub = lax.axis_index("sub")

    def at_dom(by):
        return (lax.rem(dom + by + n_dom, n_dom), sub)

    def has_dom(by):
        return dom + by >= 0 if by < 0 else dom + by < n_dom

    def at_sub(by):
        return (dom, lax.rem(sub + by + n_sub, n_sub))

    arrays = (
        (lam_in, lam_ref),
        (dom_in, dom_ref),
        (sub_in, sub_ref),
        (cnt_in, cnt_ref),
        (part_in, part_ref),
        (orient_in, orient_ref),
        (visc_in, visc_ref),
        (vel_in, vel_ref),
        (inv_in, inv_ref),
    )
    loads = [
        pltpu.make_async_copy(src, dst, in_sem.at[i]) for i, (src, dst) in enumerate(arrays)
    ]
    for load in loads:
        load.start()

    barrier = pltpu.get_barrier_semaphore()
    partners = 2
    for by in (-2, 2, -1, 1):
        partners = partners + jnp.where(has_dom(by), 1, 0)

        @pl.when(has_dom(by))
        def _(by=by):
            pl.semaphore_signal(barrier, inc=1, device_id=at_dom(by), device_id_type=MESH)

    for by in (-1, 1):
        pl.semaphore_signal(barrier, inc=1, device_id=at_sub(by), device_id_type=MESH)

    row = lax.broadcasted_iota(I32, (8, 128), 0)
    lane = lax.broadcasted_iota(I32, (8, 128), 1)
    low = row < 4
    half = jnp.where(low, 0, 1)
    left = lane < 64

    def spread(ref, r):
        return jnp.broadcast_to(ref[pl.ds(r, 1), :], (8, 128))

    def halves(ref, r, c):
        a = ref[pl.ds(r, 1), pl.ds(256 * c, 128)]
        b = ref[pl.ds(r, 1), pl.ds(256 * c + 128, 128)]
        return jnp.where(low, jnp.broadcast_to(a, (8, 128)), jnp.broadcast_to(b, (8, 128)))

    def entries(k):
        if k < 4:
            a = dom_ref[pl.ds(1 + k // 2, 1), pl.ds(128 * (k % 2), 128)]
            return jnp.broadcast_to(a, (8, 128))
        if k < 6:
            return jnp.broadcast_to(sub_ref[pl.ds(k - 4, 1), :], (8, 128))
        a = jnp.broadcast_to(dom_ref[pl.ds(0, 1), pl.ds(0, 128)], (8, 128))
        b = jnp.broadcast_to(dom_ref[pl.ds(3, 1), pl.ds(0, 128)], (8, 128))
        return jnp.where(left, a, pltpu.roll(b, 64, 1))

    def valid(k):
        if k < 4:
            return lane + 128 * (k % 2) < cnt_ref[1 + k // 2]
        if k < 6:
            return lane >= 0
        return jnp.where(left, lane, lane - 64) < jnp.where(left, cnt_ref[0], cnt_ref[3])

    for load in loads[:3]:
        load.wait()
    for k in range(7):
        e = entries(k)
        ehi[k] = lax.shift_right_logical(e, 7)
        elo[k] = lax.bitwise_and(e, 127)
    for c in range(2):
        for n in range(27):
            parts = [lam_ref[n, :, pl.ds(256 * c + 128 * h, 128)] for h in range(2)]
            xs[0, c, n] = jnp.concatenate(parts, axis=0)

    def prepare():
        for load in loads[3:]:
            load.wait()
        for c in range(2):
            mean = None
            for n in range(27):
                v = halves(visc_ref, n, c)
                vb[c, n] = v
                w = float(WEIGHTS[n // 9] * WEIGHTS[n // 3 % 3] * WEIGHTS[n % 3])
                mean = v * w if mean is None else mean + v * w
            mean = mean * 0.125
            inv = halves(inv_ref, 0, c)
            invb[c] = inv
            hmv[c] = 0.5 * mean
            for d in range(3):
                speed = halves(vel_ref, d, c)
                velb[c, d] = speed
                for s in range(2):
                    outward = speed if s == 0 else -speed
                    rate[2 * (2 * d + s) + c] = jnp.minimum(outward, 0.0) + 2.0 * (mean * inv)

        wide = lax.broadcasted_iota(I32, (128, 128), 0)
        found = jnp.zeros((48, 128), F32)
        for k in range(7):
            e = entries(k)
            hi = lax.shift_right_logical(e, 7)
            lo = lax.bitwise_and(e, 127)
            ok = valid(k)
            where_row = [jnp.where((hi == row + 8 * b) & ok, 1.0, 0.0) for b in range(3)]
            lane_f = lane.astype(F32)
            left_rows = [x * float(k + 1) for x in where_row] + [x * lane_f for x in where_row]
            a = jnp.concatenate(left_rows, axis=0).astype(jnp.bfloat16)
            b = jnp.where(jnp.concatenate([lo] * 16, axis=0) == wide, 1.0, 0.0).astype(jnp.bfloat16)
            found = found + lax.dot_general(
                a, b, (((1,), (1,)), ((), ())), preferred_element_type=F32
            )
        nat[...] = found.astype(I32)

        for f in range(6):
            for c in range(2):
                g = 2 * f + c
                ra, rb = 4 * f + 2 * c, 4 * f + 2 * c + 1
                p = jnp.where(low, spread(part_ref, ra), spread(part_ref, rb))
                r = lax.shift_right_logical(p, 7)
                swap = lax.bitwise_xor(lax.bitwise_and(r, 1), half)
                ihi[g] = swap * 12 + lax.shift_right_logical(r, 1)
                ilo[g] = lax.bitwise_and(p, 127)
                rhi[g] = jnp.where(low, spread(nat, ra), spread(nat, rb))
                rlo[g] = jnp.where(low, spread(nat, 24 + ra), spread(nat, 24 + rb))
                ori[g] = jnp.where(low, spread(orient_ref, ra), spread(orient_ref, rb))

    def put_table(f, c, values):
        g = 2 * f + c
        swapped = [pltpu.roll(x, 4, 0) for x in values]
        for q in range(9):
            tab[g, q] = values[q]
            tab[12 + g, q] = swapped[q]
        for k in range(5):
            if k < 4:
                tp[4 * f + 2 * c, k] = jnp.where(low, values[2 * k], swapped[2 * k + 1])
                tp[4 * f + 2 * c + 1, k] = jnp.where(low, swapped[2 * k], values[2 * k + 1])
            else:
                tp[4 * f + 2 * c, k] = values[8]
                tp[4 * f + 2 * c + 1, k] = swapped[8]

    def copies(rnd):
        plan = [
            (sfar.at[rnd, 0], rfar.at[rnd, 1], "dom", -2),
            (sfar.at[rnd, 1], rfar.at[rnd, 0], "dom", 2),
        ]
        for part in range(2):
            piece = pl.ds(5 * part, 5)
            plan.append((snear.at[rnd, 0, piece], rnear.at[rnd, 1, piece], "dom", -1))
            plan.append((snear.at[rnd, 1, piece], rnear.at[rnd, 0, piece], "dom", 1))
        plan.append((ssub.at[rnd, 0], rsub.at[rnd, 1], "sub", -1))
        plan.append((ssub.at[rnd, 1], rsub.at[rnd, 0], "sub", 1))
        made = []
        for i, (src, dst, axis, by) in enumerate(plan):
            copy = pltpu.make_async_remote_copy(
                src_ref=src,
                dst_ref=dst,
                send_sem=send_sem.at[rnd, i],
                recv_sem=recv_sem.at[rnd, i],
                device_id=at_dom(by) if axis == "dom" else at_sub(by),
                device_id_type=MESH,
            )
            made.append((copy, axis, by))
        return made

    def start(entry):
        copy, axis, by = entry
        if axis == "sub":
            copy.start()
        else:
            pl.when(has_dom(by))(copy.start)

    def wait_in(entry):
        copy, axis, by = entry
        if axis == "sub":
            copy.wait_recv()
        else:
            pl.when(has_dom(-by))(copy.wait_recv)

    def wait_out(entry):
        copy, axis, by = entry
        if axis == "sub":
            copy.wait_send()
        else:
            pl.when(has_dom(by))(copy.wait_send)

    def collect(k):
        hi, lo = ehi[k], elo[k]
        total = [None] * 5
        for s in range(24):
            here = hi == s
            for m in range(5):
                x = lanes(tp[s, m], lo)
                total[m] = x if s == 0 else jnp.where(here, x, total[m])
        return total

    def send(rnd):
        out = copies(rnd)
        x = collect(6)
        for m in range(3):
            a = x[2 * m]
            if m < 2:
                b = x[2 * m + 1]
                sfar[rnd, 0, m] = jnp.where(left, a, pltpu.roll(b, 64, 1))
                sfar[rnd, 1, m] = jnp.where(left, pltpu.roll(a, 64, 1), b)
            else:
                sfar[rnd, 0, m] = a
                sfar[rnd, 1, m] = pltpu.roll(a, 64, 1)

        @pl.when(rnd == 0)
        def _():
            pl.semaphore_wait(barrier, partners)

        start(out[0])
        start(out[1])
        for part in range(2):
            for side in range(2):
                x = collect(2 * side + part)
                for m in range(5):
                    snear[rnd, side, 5 * part + m] = x[m]
        for entry in out[2:6]:
            start(entry)
        for side in range(2):
            x = collect(4 + side)
            for m in range(5):
                ssub[rnd, side, m] = x[m]
        for entry in out[6:]:
            start(entry)

    def gathered(g):
        hi, lo = ihi[g], ilo[g]
        total = [None] * 9
        for s in range(24):
            here = hi == s
            for q in range(9):
                x = lanes(tab[s, q], lo)
                total[q] = x if s == 0 else jnp.where(here, x, total[q])
        return total

    def local(into):
        def groups(b, carry):
            for u in range(6):
                g = 6 * b + u
                total = gathered(g)
                for q in range(9):
                    into[g, q] = total[q]
            return carry

        lax.fori_loop(0, 2, groups, 0)

    def double(k, words):
        for m in range(5):
            x = words[m]
            y = pltpu.roll(x, 4, 0)
            dup[k, 2 * m] = jnp.where(low, x, y)
            if m < 4:
                dup[k, 2 * m + 1] = jnp.where(low, y, x)

    def merged(total, g, lists):
        hi, lo = rhi[g], rlo[g]
        for k in lists:
            here = hi == k + 1
            for q in range(9):
                total[q] = jnp.where(here, lanes(dup[k, q], lo), total[q])
        return total

    def arrive(rnd, into, difference):
        moved = copies(rnd)
        for entry in moved[6:]:
            wait_in(entry)
        for k in range(2):
            double(4 + k, [rsub[rnd, k, m] for m in range(5)])

        def merge(lists):
            for g in range(12):
                total = merged([into[g, q] for q in range(9)], g, lists)
                for q in range(9):
                    into[g, q] = total[q]

        for entry in moved[:2]:
            wait_in(entry)
        far = []
        for m in range(3):
            a, b = rfar[rnd, 0, m], rfar[rnd, 1, m]
            far.append(jnp.where(left, a, pltpu.roll(b, 64, 1)))
            if m < 2:
                far.append(jnp.where(left, pltpu.roll(a, 64, 1), b))
        double(6, far)
        merge([4, 5, 6])
        for entry in moved[2:6]:
            wait_in(entry)
        for k in range(4):
            double(k, [rnear[rnd, k // 2, 5 * (k % 2) + m] for m in range(5)])

        def last(b, carry):
            for u in range(6):
                g = 6 * b + u
                code = ori[g]
                total = merged([into[g, q] for q in range(9)], g, range(4))
                flip_i = lax.bitwise_and(code, 1) == 1
                flip_j = lax.bitwise_and(code, 2) == 2
                swap = lax.bitwise_and(code, 4) == 4
                for j in range(3):
                    x, y = total[j], total[6 + j]
                    total[j] = jnp.where(flip_i, y, x)
                    total[6 + j] = jnp.where(flip_i, x, y)
                for i in range(3):
                    x, y = total[3 * i], total[3 * i + 2]
                    total[3 * i] = jnp.where(flip_j, y, x)
                    total[3 * i + 2] = jnp.where(flip_j, x, y)
                for i in range(3):
                    for j in range(i):
                        x, y = total[3 * i + j], total[3 * j + i]
                        total[3 * i + j] = jnp.where(swap, y, x)
                        total[3 * j + i] = jnp.where(swap, x, y)
                for q in range(9):
                    own = tab[g, q]
                    into[g, q] = total[q] - own if difference else total[q] + own
            return carry

        lax.fori_loop(0, 2, last, 0)

    def segment(seg, carry):
        def traces(c, carry):
            for d in range(3):
                face = ([], [])
                for q in range(9):
                    x = [xs[seg, c, node(d, k, q)] for k in range(3)]
                    for s in range(2):
                        face[s].append(combine(ENDS[s], x))
                for s in range(2):
                    put_table(2 * d + s, c, face[s])
            return carry

        lax.fori_loop(0, 2, traces, 0)
        send(2 * seg)
        pl.when(seg == 0)(prepare)
        local(jmp)
        arrive(2 * seg, jmp, True)

        def gradients(c, carry):
            inv = invb[c]
            for d in range(3):
                face = ([], [])
                for q in range(9):
                    x = [xs[seg, c, node(d, k, q)] for k in range(3)]
                    jumps = [jmp[2 * (2 * d + s) + c, q] for s in range(2)]
                    g = []
                    for k in range(3):
                        lift = [0.5 * SIGNS[s] * ENDS[s][k] / WEIGHTS[k] for s in range(2)]
                        g.append(inv * combine(list(DERIV[k]) + lift, x + jumps))
                        grd[c, d, 3 * q + k] = g[k]
                    for s in range(2):
                        face[s].append(combine(SIGNS[s] * ENDS[s], g))
                for s in range(2):
                    put_table(2 * d + s, c, face[s])
            return carry

        lax.fori_loop(0, 2, gradients, 0)
        send(2 * seg + 1)
        local(nsum)
        arrive(2 * seg + 1, nsum, False)

        def advance(c):
            inv, drag = invb[c], hmv[c]
            total = [None] * 27
            for d in range(3):
                speed = velb[c, d]
                rates = [rate[2 * (2 * d + s) + c] for s in range(2)]
                for q in range(9):
                    flux = []
                    for k in range(3):
                        n = node(d, k, q)
                        flux.append(vb[c, n] * grd[c, d, 3 * q + k] - speed * xs[seg, c, n])
                    surface = []
                    for s in range(2):
                        g = 2 * (2 * d + s) + c
                        surface.append(rates[s] * jmp[g, q] - drag * nsum[g, q])
                    for k in range(3):
                        n = node(d, k, q)
                        lift = [ENDS[s][k] / WEIGHTS[k] for s in range(2)]
                        term = combine(list(DERIV[k]) + lift, flux + surface)
                        total[n] = term if total[n] is None else total[n] + term
            scale = STEP * inv
            for n in range(27):
                new = xs[seg, c, n] + scale * total[n]
                xs[seg + 1, c, n] = new
                result = 0.5 * (xs[0, c, n] + new)
                for h in range(2):
                    out_ref[n, :, pl.ds(256 * c + 128 * h, 128)] = result[4 * h : 4 * h + 4]

        advance(0)
        advance(1)
        return carry

    lax.fori_loop(0, 2, segment, 0)

    def drain(rnd, carry):
        for entry in copies(rnd):
            wait_out(entry)
        return carry

    lax.fori_loop(0, 4, drain, 0)


def on_device(
    n_dom,
    n_sub,
    adjoint_in,
    viscosity,
    velocity,
    inverse_size,
    local_partner,
    face_orient,
    dom_counts,
    dom_slots,
    sub_slots,
):
    lam = adjoint_in.transpose(1, 0, 2)
    vmem = pl.BlockSpec(memory_space=pltpu.VMEM)
    tile = (8, 128)
    out = pl.pallas_call(
        functools.partial(kernel, n_dom, n_sub),
        out_shape=jax.ShapeDtypeStruct((27, 4, 512), F32),
        in_specs=[pl.BlockSpec(memory_space=pl.ANY)] * 9,
        out_specs=vmem,
        scratch_shapes=[
            pltpu.VMEM((27, 4, 512), F32),
            pltpu.VMEM((27, 512), F32),
            pltpu.VMEM((3, 512), F32),
            pltpu.VMEM((1, 512), F32),
            pltpu.VMEM((24, 128), I32),
            pltpu.VMEM((24, 128), I32),
            pltpu.SMEM((4,), I32),
            pltpu.VMEM((4, 256), I32),
            pltpu.VMEM((2, 128), I32),
            pltpu.SemaphoreType.DMA((9,)),
            pltpu.VMEM((3, 2, 27) + tile, F32),
            pltpu.VMEM((2, 27) + tile, F32),
            pltpu.VMEM((2, 3) + tile, F32),
            pltpu.VMEM((2,) + tile, F32),
            pltpu.VMEM((2,) + tile, F32),
            pltpu.VMEM((12,) + tile, F32),
            pltpu.VMEM((24, 9) + tile, F32),
            pltpu.VMEM((24, 5) + tile, F32),
            pltpu.VMEM((12, 9) + tile, F32),
            pltpu.VMEM((12, 9) + tile, F32),
            pltpu.VMEM((2, 3, 27) + tile, F32),
            pltpu.VMEM((7,) + tile, I32),
            pltpu.VMEM((7,) + tile, I32),
            pltpu.VMEM((12,) + tile, I32),
            pltpu.VMEM((12,) + tile, I32),
            pltpu.VMEM((12,) + tile, I32),
            pltpu.VMEM((12,) + tile, I32),
            pltpu.VMEM((12,) + tile, I32),
            pltpu.VMEM((48, 128), I32),
            pltpu.VMEM((7, 9) + tile, F32),
            pltpu.VMEM((4, 2, 10) + tile, F32),
            pltpu.VMEM((4, 2, 5) + tile, F32),
            pltpu.VMEM((4, 2, 3) + tile, F32),
            pltpu.VMEM((4, 2, 10) + tile, F32),
            pltpu.VMEM((4, 2, 5) + tile, F32),
            pltpu.VMEM((4, 2, 3) + tile, F32),
            pltpu.SemaphoreType.DMA((4, 8)),
            pltpu.SemaphoreType.DMA((4, 8)),
        ],
        compiler_params=pltpu.CompilerParams(collective_id=0, has_side_effects=True, vmem_limit_bytes=24 << 20),
        name="segments",
    )(
        *(
            pltpu.with_memory_space_constraint(x, pltpu.HBM)
            for x in (
                lam,
                viscosity,
                velocity,
                inverse_size.reshape(1, 512),
                local_partner.reshape(24, 128),
                face_orient.reshape(24, 128),
                dom_counts.reshape(4),
                dom_slots.reshape(4, 256),
                sub_slots.reshape(2, 128),
            )
        )
    )
    return out.transpose(1, 0, 2)


def solution(mesh):
    in_specs = (
        P(None, None, ("dom", "sub")),
        P(None, ("dom", "sub")),
        P(None, ("dom", "sub")),
        P(("dom", "sub")),
        P("dom", "sub", None),
        P("dom", "sub", None),
        P("dom", "sub", None),
        P("dom", "sub", None, None),
        P("dom", "sub", None, None),
    )
    return jax.shard_map(
        functools.partial(on_device, mesh.shape["dom"], mesh.shape["sub"]),
        mesh=mesh,
        in_specs=in_specs,
        out_specs=P(None, None, ("dom", "sub")),
        check_vma=False,
    )
```
